32 devices in a mesh: ctx: 16 (over z, y, x), head: 2 (over core).
Axes of the slice: x: 2, y: 2, z: 4, core: 2. Of those that a mesh axis runs over, the one named last changes fastest.
Arguments:
- queries: bfloat16 [2048, 32, 128], P('ctx', 'head'), may hold values from -190 to 190
- keys: bfloat16 [2048, 8, 128], P('ctx', 'head'), may hold values from -6.2 to 6.2
- values: bfloat16 [2048, 8, 128], P('ctx', 'head'), may hold values from -16 to 16
- feature_weight: float32 [32, 128, 128], P('head'), may hold values from -0.5 to 0.5
Outputs:
- student: bfloat16 [2048, 32, 128], P('ctx', 'head')
- update: float32 [32, 128, 128], P('head')
The draws below stay inside these ranges and needn't reach their ends.
All inputs are finite; a program needn't handle non-finite values.
Results may differ from the reference program's by a relative error of at most 0.003.
The reference program's roundings to bfloat16 on the way count: a program that leaves them out, or rounds other values in their place, can miss the bound.
Values may be sent and summed in bfloat16 or wider, within the bound.
A program may use at most 64 MiB of HBM per device.

```python
import math
import jax
import jax.numpy as jnp
from jax import lax

HQ = 32
KVH = 8
DH = 128
DF = 64
TOK_DEV = 128
SEQ = 2048


def draw_pair(key):
    query_seed = jax.random.fold_in(key, 101)
    key_seed = jax.random.fold_in(key, 102)
    key_rows = jnp.clip(jax.random.normal(key_seed, (SEQ, KVH, DH), jnp.float32), -6.0, 6.0)
    query_rows = 1.5 * jnp.clip(jax.random.normal(query_seed, (SEQ, HQ, DH), jnp.float32), -6.0, 6.0)
    return (query_rows, key_rows)


def draw_queries(key, part):
    return draw_pair(key)[0].astype(jnp.bfloat16)


def draw_keys(key, part):
    return draw_pair(key)[1].astype(jnp.bfloat16)


def draw_values(key, part):
    noise_seed = jax.random.fold_in(key, 201)
    ladder = jnp.arange(KVH, dtype=jnp.float32) / max(KVH - 1, 1)
    noise = jnp.clip(jax.random.normal(noise_seed, (SEQ, KVH, DH), jnp.float32), -4.0, 4.0)
    head_scale = 1.0 + 2.0 * ladder
    return (noise * head_scale[None, :, None]).astype(jnp.bfloat16)


def shard_levels(rng, shape, split, smallest, high):
    factor_of, own = 1.0, jax.random.fold_in(rng, 6)
    for dim, blocks in split:
        steps = jnp.exp(jax.random.uniform(jax.random.fold_in(own, dim), (blocks,), jnp.float32, smallest / len(split), high / len(split)))
        factor_of = factor_of * jnp.repeat(steps, shape[dim] // blocks).reshape([-1 if axis == dim else 1 for axis in range(len(shape))])
    return factor_of


def bell_draw(own_key, shape, deviation, reach, shards=(), kind=jnp.bfloat16):
    loudness = shard_levels(own_key, shape, shards, -0.22, 0.18) if shards else 1.0
    drawn = jax.random.normal(own_key, shape, jnp.float32) * deviation * loudness
    return jnp.minimum(jnp.maximum(drawn, -reach), reach).astype(kind)


def setup_inputs(seed: int = 0) -> dict:
    key_of = jax.random.split(jax.random.key(seed), 5)
    return {
        "queries": draw_queries(jax.random.fold_in(key_of[4], 71), 0),
        "keys": draw_keys(jax.random.fold_in(key_of[4], 71), 0),
        "values": draw_values(jax.random.fold_in(key_of[4], 71), 0),
        "feature_weight": bell_draw(key_of[3], (HQ, DH, 2 * DF), DH ** -0.5, 0.5, ((0, 2),), jnp.float32),
    }


def feature_map(projection):
    return jnp.concatenate([jax.nn.softmax(projection, axis=-1), jax.nn.softmax(-projection, axis=-1)], axis=-1)

def teacher_head(query, key_rows, value_rows):
    count = query.shape[0]
    scores = jnp.dot(query, key_rows.T, preferred_element_type=jnp.float32) / math.sqrt(DH)
    position = jnp.arange(count, dtype=jnp.int32)
    allowed = position[None, :] <= position[:, None]
    scores = jnp.where(allowed, scores, -1e+30)
    row_max = lax.optimization_barrier(jnp.max(scores, axis=-1, keepdims=True))
    attn_weight = jnp.where(allowed, jnp.exp(scores - row_max), 0.0)
    running_sum = lax.optimization_barrier(jnp.sum(attn_weight, axis=-1, keepdims=True))
    mixed = jnp.dot(attn_weight.astype(jnp.bfloat16), value_rows, preferred_element_type=jnp.float32)
    return mixed / running_sum

def student_head(query, key_rows, value_rows, weight):
    blocks = query.shape[0] // TOK_DEV
    query_blocks = query.reshape(blocks, TOK_DEV, DH).astype(jnp.float32)
    key_blocks = key_rows.reshape(blocks, TOK_DEV, DH)
    value_blocks = value_rows.reshape(blocks, TOK_DEV, DH)
    key_before = jnp.concatenate([jnp.zeros_like(key_blocks[:1]), key_blocks[:-1]], axis=0)
    value_before = jnp.concatenate([jnp.zeros_like(value_blocks[:1]), value_blocks[:-1]], axis=0)
    window_keys = jnp.concatenate([key_before, key_blocks], axis=1).astype(jnp.float32)
    window_values = jnp.concatenate([value_before, value_blocks], axis=1).astype(jnp.float32)
    scores = jnp.einsum('btd,bsd->bts', query_blocks, window_keys) / math.sqrt(DH)
    row_index = jnp.arange(TOK_DEV, dtype=jnp.int32)
    column = jnp.arange(2 * TOK_DEV, dtype=jnp.int32)
    block_ids = jnp.arange(blocks, dtype=jnp.int32)
    earlier = (column[None, None, :] < TOK_DEV) & (block_ids[:, None, None] > 0)
    inside = (column[None, None, :] >= TOK_DEV) & (column[None, None, :] - TOK_DEV <= row_index[None, :, None])
    allowed = earlier | inside
    scores = jnp.where(allowed, scores, -1e+30)
    row_max = lax.optimization_barrier(jnp.max(scores, axis=-1))
    window_weight = jnp.where(allowed, jnp.exp(scores - row_max[..., None]), 0.0)
    window_den = lax.optimization_barrier(jnp.sum(window_weight, axis=-1))
    rounded = lax.optimization_barrier(window_weight.astype(jnp.bfloat16))
    window_num = jnp.einsum('bts,bsd->btd', rounded.astype(jnp.float32), window_values)
    query_feat = feature_map(jnp.dot(query.astype(jnp.float32), weight[:, :DF], precision=lax.Precision.HIGHEST))
    query_feat = query_feat.reshape(blocks, TOK_DEV, 2 * DF)
    key_feat = feature_map(jnp.dot(key_rows.astype(jnp.float32), weight[:, DF:], precision=lax.Precision.HIGHEST))
    key_feat = key_feat.reshape(blocks, TOK_DEV, 2 * DF)
    own_state = jnp.einsum('btf,btd->bfd', key_feat, value_blocks.astype(jnp.float32), precision=lax.Precision.HIGHEST)
    own_norm = lax.optimization_barrier(jnp.sum(key_feat, axis=1))
    run_state = jnp.cumsum(own_state, axis=0)
    run_norm = jnp.cumsum(own_norm, axis=0)
    state = jnp.concatenate([jnp.zeros_like(run_state[:2]), run_state[:-2]], axis=0)
    norm = jnp.concatenate([jnp.zeros_like(run_norm[:2]), run_norm[:-2]], axis=0)
    decay = jnp.exp(-row_max)
    far_num = decay[..., None] * jnp.einsum('btf,bfd->btd', query_feat, state, precision=lax.Precision.HIGHEST)
    far_den = decay * jnp.einsum('btf,bf->bt', query_feat, norm, precision=lax.Precision.HIGHEST)
    mix = (window_num + far_num) / (window_den + far_den)[..., None]
    return mix.reshape(blocks * TOK_DEV, DH)

def reference(queries, keys, values, feature_weight):
    group_size = HQ // KVH

    def per_head(head_id):
        kv_id = head_id // group_size
        query = lax.dynamic_index_in_dim(queries, head_id, 1, keepdims=False)
        key_rows = lax.dynamic_index_in_dim(keys, kv_id, 1, keepdims=False)
        value_rows = lax.dynamic_index_in_dim(values, kv_id, 1, keepdims=False)
        weight = lax.dynamic_index_in_dim(feature_weight, head_id, 0, keepdims=False)
        teacher = teacher_head(query, key_rows, value_rows)

        def student_of(weight_in):
            return student_head(query, key_rows, value_rows, weight_in)
        mix, pull_back = jax.vjp(student_of, weight)
        gradient = pull_back(mix - teacher)[0]
        return (mix.astype(jnp.bfloat16), gradient)
    mixes, gradients = lax.map(per_head, jnp.arange(HQ, dtype=jnp.int32))
    student = jnp.transpose(mixes, (1, 0, 2))
    update = gradients / jnp.sqrt(jnp.mean(gradients * gradients) + 1e-06)
    return (student, update)
```

```python
import functools
import math

import jax
import jax.numpy as jnp
from jax import lax
from jax.experimental import pallas as pl
from jax.experimental.pallas import tpu as pltpu
from jax.sharding import PartitionSpec as P

precise = lax.Precision.HIGHEST
big_negative = -1e30


def shifted(shard, axis, by):
    devices = lax.axis_size(axis)
    pairs = [(i, i + by) for i in range(devices) if 0 <= i + by < devices]
    return lax.ppermute(shard, axis, pairs)


def carried_in(part, axis, combine, identity):
    count = lax.axis_size(axis)
    place = lax.axis_index(axis)
    ahead = count - 1 - place
    gathered = jax.tree.map(lambda a: lax.all_gather(a, axis), part)
    state = jax.tree.map(lambda a, e: jnp.zeros_like(a) + jnp.asarray(e, a.dtype), part, identity)

    def one(step, state):
        source = count - 1 - step
        return combine(
            state, jax.tree.map(lambda a: lax.dynamic_index_in_dim(a, source, 0, False), gathered)
        )

    return lax.fori_loop(0, ahead, one, state)


def feature_map(projection):
    return jnp.concatenate(
        [jax.nn.softmax(projection, axis=-1), jax.nn.softmax(-projection, axis=-1)], axis=-1
    )


def feature_pull(projection, upstream):
    half_len = upstream.shape[-1] // 2
    upper = jax.nn.softmax(projection, axis=-1)
    lower = jax.nn.softmax(-projection, axis=-1)
    grad_upper = upstream[..., :half_len]
    grad_lower = upstream[..., half_len:]
    upper_part = upper * (grad_upper - jnp.sum(upper * grad_upper, axis=-1, keepdims=True))
    lower_part = lower * (grad_lower - jnp.sum(lower * grad_lower, axis=-1, keepdims=True))
    return upper_part - lower_part


def add_pair(earlier, later):
    return (earlier[0] + later[0], earlier[1] + later[1])


def skip_block(carry_in):
    return carry_in


def general_shards(queries, keys, values, feature_weight):
    block_len, head_count, head_width = queries.shape
    kv_count = keys.shape[1]
    group_size = head_count // kv_count
    feature_len = feature_weight.shape[2] // 2
    my_block = lax.axis_index("ctx")
    score_scale = 1.0 / math.sqrt(head_width)
    grouped_q = queries.reshape(block_len, kv_count, group_size, head_width)
    maps_weight = feature_weight.reshape(kv_count, group_size, head_width, 2 * feature_len)
    query_map = maps_weight[..., :feature_len]
    key_map = maps_weight[..., feature_len:]
    query_pos = my_block * block_len + jnp.arange(block_len, dtype=jnp.int32)
    prev_start = (my_block - 1) * block_len
    last_row = my_block * block_len + block_len - 1
    initial = [
        jnp.full((kv_count, group_size, block_len), big_negative, jnp.float32),
        jnp.zeros((kv_count, group_size, block_len), jnp.float32),
        jnp.zeros((kv_count, group_size, block_len, head_width), jnp.float32),
    ]
    initial = initial + [
        jnp.zeros((kv_count, group_size, 2 * feature_len, head_width), jnp.float32),
        jnp.zeros((kv_count, group_size, 2 * feature_len), jnp.float32),
    ]
    initial = tuple(initial)
    piece_keys = lax.all_gather(keys, "ctx", axis=0, tiled=True)
    piece_values = lax.all_gather(values, "ctx", axis=0, tiled=True)
    piece_rows = piece_keys.shape[0]
    step_rows = math.gcd(piece_rows, 512)

    def attend(step_index, running):
        first_row = step_index * step_rows
        block_keys = lax.dynamic_slice_in_dim(piece_keys, step_index * step_rows, step_rows, 0)
        block_values = lax.dynamic_slice_in_dim(piece_values, step_index * step_rows, step_rows, 0)
        key_pos = first_row + jnp.arange(step_rows, dtype=jnp.int32)

        def compute(carry_in):
            row_max, running_sum, accumulated = (carry_in[0], carry_in[1], carry_in[2])
            scores = (
                jnp.einsum(
                    "tkgd,skd->kgts", grouped_q, block_keys, preferred_element_type=jnp.float32
                )
                * score_scale
            )
            allowed = key_pos[None, :] <= query_pos[:, None]
            scores = jnp.where(allowed, scores, big_negative)
            new_max = jnp.maximum(row_max, jnp.max(scores, axis=-1))
            attn_weight = jnp.where(allowed, jnp.exp(scores - new_max[..., None]), 0.0)
            factor = jnp.exp(row_max - new_max)
            running_sum = running_sum * factor + jnp.sum(attn_weight, axis=-1)
            accumulated = accumulated * factor[..., None] + jnp.einsum(
                "kgts,skd->kgtd",
                attn_weight.astype(jnp.bfloat16),
                block_values,
                preferred_element_type=jnp.float32,
            )
            result = [new_max, running_sum, accumulated] + list(carry_in[3:])
            in_state = (key_pos < prev_start).astype(jnp.float32)
            features = feature_map(
                jnp.einsum(
                    "skd,kgdf->kgsf", block_keys.astype(jnp.float32), key_map, precision=precise
                )
            )
            features = features * in_state[None, None, :, None]
            result[-2] = carry_in[-2] + jnp.einsum(
                "kgsf,skd->kgfd", features, block_values.astype(jnp.float32), precision=precise
            )
            result[-1] = carry_in[-1] + jnp.sum(features, axis=2)
            return tuple(result)

        return lax.cond(first_row <= last_row, compute, skip_block, running)

    folded = lax.fori_loop(0, piece_rows // step_rows, attend, initial)
    teacher = folded[2] / folded[1][..., None]
    stacked = jnp.stack([keys, values])
    moved = shifted(stacked, "ctx", 1)
    prev_keys, prev_values = (moved[0], moved[1])
    has_prev = (my_block > 0).astype(jnp.float32)
    window_keys = jnp.concatenate([prev_keys, keys], axis=0)
    window_values = jnp.concatenate([prev_values, values], axis=0)
    column = jnp.arange(2 * block_len, dtype=jnp.int32)
    row_index = jnp.arange(block_len, dtype=jnp.int32)
    allowed = (column[None, :] < block_len) & (my_block > 0) | (column[None, :] >= block_len) & (
        column[None, :] - block_len <= row_index[:, None]
    )
    scores = (
        jnp.einsum("tkgd,skd->kgts", grouped_q, window_keys, preferred_element_type=jnp.float32)
        * score_scale
    )
    scores = jnp.where(allowed, scores, big_negative)
    row_max = jnp.max(scores, axis=-1)
    window_weight = jnp.where(allowed, jnp.exp(scores - row_max[..., None]), 0.0)
    window_den = jnp.sum(window_weight, axis=-1)
    window_num = jnp.einsum(
        "kgts,skd->kgtd",
        window_weight.astype(jnp.bfloat16),
        window_values,
        preferred_element_type=jnp.float32,
    )
    key_proj = jnp.einsum(
        "skd,kgdf->kgsf", prev_keys.astype(jnp.float32), key_map, precision=precise
    )
    state, norm = (folded[-2], folded[-1])
    query_proj = jnp.einsum(
        "tkgd,kgdf->kgtf", grouped_q.astype(jnp.float32), query_map, precision=precise
    )
    query_feats = feature_map(query_proj)
    decay = jnp.exp(-row_max)
    far_num = decay[..., None] * jnp.einsum(
        "kgtf,kgfd->kgtd", query_feats, state, precision=precise
    )
    far_den = decay * jnp.einsum("kgtf,kgf->kgt", query_feats, norm, precision=precise)
    denominator = window_den + far_den
    mix = (window_num + far_num) / denominator[..., None]
    student = jnp.transpose(mix.astype(jnp.bfloat16), (2, 0, 1, 3)).reshape(
        block_len, head_count, head_width
    )
    mismatch = mix - teacher
    grad_num = mismatch / denominator[..., None]
    grad_den = -jnp.sum(mismatch * mix, axis=-1) / denominator
    lifted = decay[..., None] * query_feats
    grad_state = jnp.einsum("kgtf,kgtd->kgfd", lifted, grad_num, precision=precise)
    grad_norm = jnp.einsum("kgtf,kgt->kgf", lifted, grad_den, precision=precise)
    grad_qfeat = decay[..., None] * (
        jnp.einsum("kgfd,kgtd->kgtf", state, grad_num, precision=precise)
        + norm[:, :, None, :] * grad_den[..., None]
    )
    later_state, later_norm = carried_in(
        (grad_state, grad_norm),
        "ctx",
        add_pair,
        (jnp.zeros_like(grad_state), jnp.zeros_like(grad_norm)),
    )
    grad_kfeat = (
        jnp.einsum(
            "kgfd,skd->kgsf", later_state, prev_values.astype(jnp.float32), precision=precise
        )
        + later_norm[:, :, None, :]
    ) * has_prev
    grad_query = jnp.einsum(
        "tkgd,kgtf->kgdf",
        grouped_q.astype(jnp.float32),
        feature_pull(query_proj, grad_qfeat),
        precision=precise,
    )
    grad_key = jnp.einsum(
        "skd,kgsf->kgdf",
        prev_keys.astype(jnp.float32),
        feature_pull(key_proj, grad_kfeat),
        precision=precise,
    )
    gradients = jnp.concatenate([grad_query, grad_key], axis=-1).reshape(
        head_count, head_width, 2 * feature_len
    )
    entry_count = gradients.size * lax.axis_size("head")
    summed = lax.psum(gradients, "ctx")
    squares = lax.psum(jnp.sum(summed * summed), "head")
    update = summed / jnp.sqrt(squares / entry_count + 1e-06)
    return (student, update)


f32, bf16 = jnp.float32, jnp.bfloat16
NN = (((1,), (0,)), ((), ()))
NT = (((1,), (1,)), ((), ()))
TN = (((0,), (0,)), ((), ()))


def mxu(a, b, dims):
    return lax.dot_general(a, b, dims, preferred_element_type=f32)


def split(x, pieces):
    out = []
    for _ in range(pieces):
        piece = x.astype(bf16)
        out.append(piece)
        x = x - piece.astype(f32)
    return out


def cat(parts, axis):
    return jnp.concatenate(parts, axis=axis)


def exact_by_wide(a, b, dims):
    return mxu(cat([a, a], dims[0][0][0]), cat(split(b, 2), dims[0][1][0]), dims)


def wide_by_exact(a, b, dims):
    return mxu(cat(split(a, 2), dims[0][0][0]), cat([b, b], dims[0][1][0]), dims)


def wide_by_wide(a, b, dims):
    a_hi, a_lo = split(a, 2)
    b_hi, b_lo = split(b, 2)
    return mxu(
        cat([a_hi, a_hi, a_lo], dims[0][0][0]), cat([b_hi, b_lo, b_hi], dims[0][1][0]), dims
    )


def half_sum(x, halves):
    return wide_by_exact(x, halves, NN)


def half_softmax(u, is_upper, halves):
    top = jnp.max(jnp.where(is_upper, u, big_negative), axis=-1, keepdims=True)
    low = jnp.max(jnp.where(is_upper, big_negative, u), axis=-1, keepdims=True)
    e = jnp.exp(u - jnp.where(is_upper, top, low))
    return e / half_sum(e, halves)


def head_kernel(
    x_ref, w_ref, student_ref, grad_ref,
    score_ref, kfeat_ref, gstate_ref, gnorm_ref, state_ref, norm_ref, last_ref, lastn_ref,
    wq_ref, wk_ref, acc_ref, peak_ref, total_ref, gq_ref, gk_ref,
):
    blocks, _, length, width = x_ref.shape
    features = w_ref.shape[1] // 2
    rows = 2 * length
    steps = blocks // 2
    scale = 1.0 / math.sqrt(width)
    lane = lax.broadcasted_iota(jnp.int32, (rows, 2 * features), 1)
    is_upper = lane < features
    row_half = lax.broadcasted_iota(jnp.int32, (2 * features, 2 * features), 0) < features
    col_half = lax.broadcasted_iota(jnp.int32, (2 * features, 2 * features), 1) < features
    halves = jnp.where(row_half == col_half, 1.0, 0.0).astype(bf16)
    w = w_ref[...]
    wq, wk = w[:, :features], w[:, features:]
    wq_ref[...] = cat(split(cat([wq, -wq], 1), 3), 0)
    wk_ref[...] = cat(split(cat([wk, -wk], 1), 3), 0)
    for ref in (state_ref, norm_ref, last_ref, lastn_ref, gq_ref, gk_ref):
        ref[...] = jnp.zeros_like(ref)

    def load(part, i):
        return x_ref[pl.ds(2 * i, 2), part].reshape(rows, width)

    def forward(i, carry):
        q, k, v = load(0, i), load(1, i), load(2, i)
        acc_ref[...] = jnp.zeros_like(acc_ref)
        total_ref[...] = jnp.zeros_like(total_ref)
        peak_ref[...] = jnp.full(peak_ref.shape, big_negative, f32)

        def score(j, carry):
            s = mxu(q, load(1, j), NT) * scale
            score_ref[j] = s
            peak_ref[...] = jnp.maximum(
                peak_ref[...], jnp.maximum(s[:, :length], s[:, length:])
            )
            return carry

        lax.fori_loop(0, i, score, 0)
        s = mxu(q, k, NT) * scale
        causal = lax.broadcasted_iota(jnp.int32, (rows, rows), 1) <= lax.broadcasted_iota(
            jnp.int32, (rows, rows), 0
        )
        s = jnp.where(causal, s, big_negative)
        score_ref[i] = s
        row_max = jnp.max(
            jnp.maximum(peak_ref[...], jnp.maximum(s[:, :length], s[:, length:])),
            axis=-1,
            keepdims=True,
        )

        def weigh(j, carry):
            p = jnp.exp(score_ref[j] - row_max)
            total_ref[...] += p[:, :length] + p[:, length:]
            acc_ref[...] += mxu(p.astype(bf16), load(2, j), NN)
            return carry

        lax.fori_loop(0, i + 1, weigh, 0)
        teacher = acc_ref[...] / jnp.sum(total_ref[...], axis=-1, keepdims=True)

        before = jnp.maximum(i - 1, 0)
        prev_top = score_ref[before, :length, length:]
        prev_top = jnp.where(i > 0, prev_top, big_negative)
        prev = cat([prev_top, s[length:, :length]], 0)
        own = cat([s[:length, :length], s[length:, length:]], 0)
        win_max = jnp.max(jnp.maximum(prev, own), axis=-1, keepdims=True)
        p_prev, p_own = jnp.exp(prev - win_max), jnp.exp(own - win_max)
        win_den = jnp.sum(p_prev + p_own, axis=-1, keepdims=True)
        b_prev, b_own = p_prev.astype(bf16), p_own.astype(bf16)
        v_before = x_ref[jnp.maximum(2 * i - 1, 0), 2]
        win_num = cat(
            [
                mxu(cat([b_prev[:length], b_own[:length]], 1), cat([v_before, v[:length]], 0), NN),
                mxu(cat([b_prev[length:], b_own[length:]], 1), v, NN),
            ],
            0,
        )

        qf = half_softmax(mxu(cat([q, q, q], 1), wq_ref[...], NN), is_upper, halves)
        kf = half_softmax(mxu(cat([k, k, k], 1), wk_ref[...], NN), is_upper, halves)
        kfeat_ref[i] = kf
        own_0 = wide_by_exact(kf[:length], v[:length], TN)
        own_1 = wide_by_exact(kf[length:], v[length:], TN)
        sum_0 = jnp.sum(kf[:length], axis=0, keepdims=True)
        sum_1 = jnp.sum(kf[length:], axis=0, keepdims=True)
        state_0, norm_0 = state_ref[...], norm_ref[...]
        state_1, norm_1 = state_0 + last_ref[...], norm_0 + lastn_ref[...]
        state_ref[...], norm_ref[...] = state_1 + own_0, norm_1 + sum_0
        last_ref[...], lastn_ref[...] = own_1, sum_1

        norm = cat(
            [
                jnp.broadcast_to(norm_0, (length, 2 * features)),
                jnp.broadcast_to(norm_1, (length, 2 * features)),
            ],
            0,
        )
        decay = jnp.exp(-win_max)
        far = cat(
            [wide_by_wide(qf[:length], state_0, NN), wide_by_wide(qf[length:], state_1, NN)], 0
        )
        den = win_den + decay * jnp.sum(qf * norm, axis=-1, keepdims=True)
        mix = (win_num + decay * far) / den
        student_ref[pl.ds(2 * i, 2)] = mix.astype(bf16).reshape(2, length, width)
        mismatch = mix - teacher
        g_num = mismatch / den
        g_den = -jnp.sum(mismatch * mix, axis=-1, keepdims=True) / den
        lifted = decay * qf
        gstate_ref[2 * i] = wide_by_wide(lifted[:length], g_num[:length], TN)
        gstate_ref[2 * i + 1] = wide_by_wide(lifted[length:], g_num[length:], TN)
        pulled_norm = lifted * g_den
        gnorm_ref[2 * i] = jnp.sum(pulled_norm[:length], axis=0, keepdims=True)
        gnorm_ref[2 * i + 1] = jnp.sum(pulled_norm[length:], axis=0, keepdims=True)
        g_qf = decay * (
            cat(
                [
                    wide_by_wide(g_num[:length], state_0, NT),
                    wide_by_wide(g_num[length:], state_1, NT),
                ],
                0,
            )
            + norm * g_den
        )
        d_q = qf * (g_qf - half_sum(qf * g_qf, halves))
        gq_ref[...] += exact_by_wide(q, d_q, TN)
        return carry

    lax.fori_loop(0, steps, forward, 0)

    for ref in (state_ref, norm_ref):
        ref[...] = jnp.zeros_like(ref)

    def backward(step, carry):
        i = steps - 1 - step
        k, v, kf = load(1, i), load(2, i), kfeat_ref[i]
        nxt = jnp.minimum(i + 1, steps - 1)
        live = jnp.where(step > 0, 1.0, 0.0)
        later_1, later_n1 = state_ref[...], norm_ref[...]
        later_0 = later_1 + live * gstate_ref[2 * nxt]
        later_n0 = later_n1 + live * gnorm_ref[2 * nxt]
        g_kf = cat(
            [
                exact_by_wide(v[:length], later_0, NT) + later_n0,
                exact_by_wide(v[length:], later_1, NT) + later_n1,
            ],
            0,
        )
        d_k = kf * (g_kf - half_sum(kf * g_kf, halves))
        gk_ref[...] += exact_by_wide(k, d_k, TN)
        state_ref[...] = later_0 + gstate_ref[2 * i + 1]
        norm_ref[...] = later_n0 + gnorm_ref[2 * i + 1]
        return carry

    lax.fori_loop(0, steps, backward, 0)
    gq, gk = gq_ref[...], gk_ref[...]
    grad_ref[...] = cat(
        [gq[:, :features] - gq[:, features:], gk[:, :features] - gk[:, features:]], 1
    )


def whole_head(x, w):
    blocks, _, length, width = x.shape
    double = w.shape[1]
    rows, steps = 2 * length, blocks // 2
    vmem = pltpu.VMEM
    return pl.pallas_call(
        head_kernel,
        out_shape=(
            jax.ShapeDtypeStruct((blocks, length, width), bf16),
            jax.ShapeDtypeStruct((width, double), f32),
        ),
        in_specs=[pl.BlockSpec(memory_space=vmem)] * 2,
        out_specs=(pl.BlockSpec(memory_space=vmem),) * 2,
        scratch_shapes=[
            vmem((steps, rows, rows), f32),
            vmem((steps, rows, double), f32),
            vmem((blocks, double, width), f32),
            vmem((blocks, 1, double), f32),
            vmem((double, width), f32),
            vmem((1, double), f32),
            vmem((double, width), f32),
            vmem((1, double), f32),
            vmem((3 * width, double), bf16),
            vmem((3 * width, double), bf16),
            vmem((rows, width), f32),
            vmem((rows, length), f32),
            vmem((rows, length), f32),
            vmem((width, double), f32),
            vmem((width, double), f32),
        ],
        compiler_params=pltpu.CompilerParams(vmem_limit_bytes=40 * 2**20),
    )(x, w)


def head_shards(queries, keys, values, feature_weight):
    block_len, head_count, head_width = queries.shape
    group = head_count // keys.shape[1]
    q = jnp.transpose(queries, (1, 0, 2))
    k = jnp.repeat(jnp.transpose(keys, (1, 0, 2)), group, axis=0)
    v = jnp.repeat(jnp.transpose(values, (1, 0, 2)), group, axis=0)
    x = lax.all_to_all(jnp.stack([q, k, v], axis=1), "ctx", 0, 0)
    w = lax.dynamic_index_in_dim(feature_weight, lax.axis_index("ctx"), 0, False)
    mix, grad = whole_head(x, w)
    student = jnp.transpose(lax.all_to_all(mix, "ctx", 0, 0), (1, 0, 2))
    squares = lax.psum(jnp.sum(grad * grad), ("ctx", "head"))
    gradients = lax.all_gather(grad, "ctx", axis=0)
    entry_count = gradients.size * lax.axis_size("head")
    update = gradients / jnp.sqrt(squares / entry_count + 1e-06)
    return (student, update)


def shards(queries, keys, values, feature_weight):
    count = lax.axis_size("ctx")
    width = queries.shape[2]
    fits = queries.shape[1] == count and count % 2 == 0 and count * queries.shape[0] <= 4096
    fits = fits and queries.shape[0] == width and feature_weight.shape[2] == width
    body = head_shards if fits else general_shards
    return body(queries, keys, values, feature_weight)


def solution(mesh):
    return jax.shard_map(
        shards,
        mesh=mesh,
        in_specs=(
            P("ctx", "head", None),
            P("ctx", "head", None),
            P("ctx", "head", None),
            P("head", None, None),
        ),
        out_specs=(P("ctx", "head", None), P("head", None, None)),
        check_vma=False,
    )
```

```python
import functools
import math

import jax
import jax.numpy as jnp
from jax import lax
from jax.experimental import pallas as pl
from jax.experimental.pallas import tpu as pltpu
from jax.sharding import PartitionSpec as P

precise = lax.Precision.HIGHEST
big_negative = -1e30


def shifted(shard, axis, by):
    devices = lax.axis_size(axis)
    pairs = [(i, i + by) for i in range(devices) if 0 <= i + by < devices]
    return lax.ppermute(shard, axis, pairs)


def carried_in(part, axis, combine, identity):
    count = lax.axis_size(axis)
    place = lax.axis_index(axis)
    ahead = count - 1 - place
    gathered = jax.tree.map(lambda a: lax.all_gather(a, axis), part)
    state = jax.tree.map(lambda a, e: jnp.zeros_like(a) + jnp.asarray(e, a.dtype), part, identity)

    def one(step, state):
        source = count - 1 - step
        return combine(
            state, jax.tree.map(lambda a: lax.dynamic_index_in_dim(a, source, 0, False), gathered)
        )

    return lax.fori_loop(0, ahead, one, state)


def feature_map(projection):
    return jnp.concatenate(
        [jax.nn.softmax(projection, axis=-1), jax.nn.softmax(-projection, axis=-1)], axis=-1
    )


def feature_pull(projection, upstream):
    half_len = upstream.shape[-1] // 2
    upper = jax.nn.softmax(projection, axis=-1)
    lower = jax.nn.softmax(-projection, axis=-1)
    grad_upper = upstream[..., :half_len]
    grad_lower = upstream[..., half_len:]
    upper_part = upper * (grad_upper - jnp.sum(upper * grad_upper, axis=-1, keepdims=True))
    lower_part = lower * (grad_lower - jnp.sum(lower * grad_lower, axis=-1, keepdims=True))
    return upper_part - lower_part


def add_pair(earlier, later):
    return (earlier[0] + later[0], earlier[1] + later[1])


def skip_block(carry_in):
    return carry_in


def general_shards(queries, keys, values, feature_weight):
    block_len, head_count, head_width = queries.shape
    kv_count = keys.shape[1]
    group_size = head_count // kv_count
    feature_len = feature_weight.shape[2] // 2
    my_block = lax.axis_index("ctx")
    score_scale = 1.0 / math.sqrt(head_width)
    grouped_q = queries.reshape(block_len, kv_count, group_size, head_width)
    maps_weight = feature_weight.reshape(kv_count, group_size, head_width, 2 * feature_len)
    query_map = maps_weight[..., :feature_len]
    key_map = maps_weight[..., feature_len:]
    query_pos = my_block * block_len + jnp.arange(block_len, dtype=jnp.int32)
    prev_start = (my_block - 1) * block_len
    last_row = my_block * block_len + block_len - 1
    initial = [
        jnp.full((kv_count, group_size, block_len), big_negative, jnp.float32),
        jnp.zeros((kv_count, group_size, block_len), jnp.float32),
        jnp.zeros((kv_count, group_size, block_len, head_width), jnp.float32),
    ]
    initial = initial + [
        jnp.zeros((kv_count, group_size, 2 * feature_len, head_width), jnp.float32),
        jnp.zeros((kv_count, group_size, 2 * feature_len), jnp.float32),
    ]
    initial = tuple(initial)
    piece_keys = lax.all_gather(keys, "ctx", axis=0, tiled=True)
    piece_values = lax.all_gather(values, "ctx", axis=0, tiled=True)
    piece_rows = piece_keys.shape[0]
    step_rows = math.gcd(piece_rows, 512)

    def attend(step_index, running):
        first_row = step_index * step_rows
        block_keys = lax.dynamic_slice_in_dim(piece_keys, step_index * step_rows, step_rows, 0)
        block_values = lax.dynamic_slice_in_dim(piece_values, step_index * step_rows, step_rows, 0)
        key_pos = first_row + jnp.arange(step_rows, dtype=jnp.int32)

        def compute(carry_in):
            row_max, running_sum, accumulated = (carry_in[0], carry_in[1], carry_in[2])
            scores = (
                jnp.einsum(
                    "tkgd,skd->kgts", grouped_q, block_keys, preferred_element_type=jnp.float32
                )
                * score_scale
            )
            allowed = key_pos[None, :] <= query_pos[:, None]
            scores = jnp.where(allowed, scores, big_negative)
            new_max = jnp.maximum(row_max, jnp.max(scores, axis=-1))
            attn_weight = jnp.where(allowed, jnp.exp(scores - new_max[..., None]), 0.0)
            factor = jnp.exp(row_max - new_max)
            running_sum = running_sum * factor + jnp.sum(attn_weight, axis=-1)
            accumulated = accumulated * factor[..., None] + jnp.einsum(
                "kgts,skd->kgtd",
                attn_weight.astype(jnp.bfloat16),
                block_values,
                preferred_element_type=jnp.float32,
            )
            result = [new_max, running_sum, accumulated] + list(carry_in[3:])
            in_state = (key_pos < prev_start).astype(jnp.float32)
            features = feature_map(
                jnp.einsum(
                    "skd,kgdf->kgsf", block_keys.astype(jnp.float32), key_map, precision=precise
                )
            )
            features = features * in_state[None, None, :, None]
            result[-2] = carry_in[-2] + jnp.einsum(
                "kgsf,skd->kgfd", features, block_values.astype(jnp.float32), precision=precise
            )
            result[-1] = carry_in[-1] + jnp.sum(features, axis=2)
            return tuple(result)

        return lax.cond(first_row <= last_row, compute, skip_block, running)

    folded = lax.fori_loop(0, piece_rows // step_rows, attend, initial)
    teacher = folded[2] / folded[1][..., None]
    stacked = jnp.stack([keys, values])
    moved = shifted(stacked, "ctx", 1)
    prev_keys, prev_values = (moved[0], moved[1])
    has_prev = (my_block > 0).astype(jnp.float32)
    window_keys = jnp.concatenate([prev_keys, keys], axis=0)
    window_values = jnp.concatenate([prev_values, values], axis=0)
    column = jnp.arange(2 * block_len, dtype=jnp.int32)
    row_index = jnp.arange(block_len, dtype=jnp.int32)
    allowed = (column[None, :] < block_len) & (my_block > 0) | (column[None, :] >= block_len) & (
        column[None, :] - block_len <= row_index[:, None]
    )
    scores = (
        jnp.einsum("tkgd,skd->kgts", grouped_q, window_keys, preferred_element_type=jnp.float32)
        * score_scale
    )
    scores = jnp.where(allowed, scores, big_negative)
    row_max = jnp.max(scores, axis=-1)
    window_weight = jnp.where(allowed, jnp.exp(scores - row_max[..., None]), 0.0)
    window_den = jnp.sum(window_weight, axis=-1)
    window_num = jnp.einsum(
        "kgts,skd->kgtd",
        window_weight.astype(jnp.bfloat16),
        window_values,
        preferred_element_type=jnp.float32,
    )
    key_proj = jnp.einsum(
        "skd,kgdf->kgsf", prev_keys.astype(jnp.float32), key_map, precision=precise
    )
    state, norm = (folded[-2], folded[-1])
    query_proj = jnp.einsum(
        "tkgd,kgdf->kgtf", grouped_q.astype(jnp.float32), query_map, precision=precise
    )
    query_feats = feature_map(query_proj)
    decay = jnp.exp(-row_max)
    far_num = decay[..., None] * jnp.einsum(
        "kgtf,kgfd->kgtd", query_feats, state, precision=precise
    )
    far_den = decay * jnp.einsum("kgtf,kgf->kgt", query_feats, norm, precision=precise)
    denominator = window_den + far_den
    mix = (window_num + far_num) / denominator[..., None]
    student = jnp.transpose(mix.astype(jnp.bfloat16), (2, 0, 1, 3)).reshape(
        block_len, head_count, head_width
    )
    mismatch = mix - teacher
    grad_num = mismatch / denominator[..., None]
    grad_den = -jnp.sum(mismatch * mix, axis=-1) / denominator
    lifted = decay[..., None] * query_feats
    grad_state = jnp.einsum("kgtf,kgtd->kgfd", lifted, grad_num, precision=precise)
    grad_norm = jnp.einsum("kgtf,kgt->kgf", lifted, grad_den, precision=precise)
    grad_qfeat = decay[..., None] * (
        jnp.einsum("kgfd,kgtd->kgtf", state, grad_num, precision=precise)
        + norm[:, :, None, :] * grad_den[..., None]
    )
    later_state, later_norm = carried_in(
        (grad_state, grad_norm),
        "ctx",
        add_pair,
        (jnp.zeros_like(grad_state), jnp.zeros_like(grad_norm)),
    )
    grad_kfeat = (
        jnp.einsum(
            "kgfd,skd->kgsf", later_state, prev_values.astype(jnp.float32), precision=precise
        )
        + later_norm[:, :, None, :]
    ) * has_prev
    grad_query = jnp.einsum(
        "tkgd,kgtf->kgdf",
        grouped_q.astype(jnp.float32),
        feature_pull(query_proj, grad_qfeat),
        precision=precise,
    )
    grad_key = jnp.einsum(
        "skd,kgsf->kgdf",
        prev_keys.astype(jnp.float32),
        feature_pull(key_proj, grad_kfeat),
        precision=precise,
    )
    gradients = jnp.concatenate([grad_query, grad_key], axis=-1).reshape(
        head_count, head_width, 2 * feature_len
    )
    entry_count = gradients.size * lax.axis_size("head")
    summed = lax.psum(gradients, "ctx")
    squares = lax.psum(jnp.sum(summed * summed), "head")
    update = summed / jnp.sqrt(squares / entry_count + 1e-06)
    return (student, update)


f32, bf16 = jnp.float32, jnp.bfloat16
NN = (((1,), (0,)), ((), ()))
NT = (((1,), (1,)), ((), ()))
TN = (((0,), (0,)), ((), ()))


def mxu(a, b, dims):
    return lax.dot_general(a, b, dims, preferred_element_type=f32)


def split(x, pieces):
    out = []
    for _ in range(pieces):
        piece = x.astype(bf16)
        out.append(piece)
        x = x - piece.astype(f32)
    return out


def cat(parts, axis):
    return jnp.concatenate(parts, axis=axis)


def exact_by_wide(a, b, dims):
    return mxu(cat([a, a], dims[0][0][0]), cat(split(b, 2), dims[0][1][0]), dims)


def wide_by_exact(a, b, dims):
    return mxu(cat(split(a, 2), dims[0][0][0]), cat([b, b], dims[0][1][0]), dims)


def wide_by_wide(a, b, dims):
    a_hi, a_lo = split(a, 2)
    b_hi, b_lo = split(b, 2)
    return mxu(
        cat([a_hi, a_hi, a_lo], dims[0][0][0]), cat([b_hi, b_lo, b_hi], dims[0][1][0]), dims
    )


def half_sum(x, halves):
    return wide_by_exact(x, halves, NN)


def half_softmax(u, is_upper, halves):
    top = jnp.max(jnp.where(is_upper, u, big_negative), axis=-1, keepdims=True)
    low = jnp.max(jnp.where(is_upper, big_negative, u), axis=-1, keepdims=True)
    e = jnp.exp(u - jnp.where(is_upper, top, low))
    return e / half_sum(e, halves)


def remote(src, dst, send_sem, recv_sem, **where):
    return pltpu.make_async_remote_copy(
        src_ref=src,
        dst_ref=dst,
        send_sem=send_sem,
        recv_sem=recv_sem,
        device_id=where,
        device_id_type=pl.DeviceIdType.MESH,
    )


def each(count, body):
    def step(index, carry):
        body(index)
        return carry

    lax.fori_loop(0, count, step, 0)


def head_kernel(
    qt_ref, kvt_ref, w_ref, student_ref, update_ref,
    q_all, kv_all, mix_ref, gat_ref, sq_ref,
    score_ref, kfeat_ref, gstate_ref, gnorm_ref, state_ref, norm_ref, last_ref, lastn_ref,
    wq_ref, wk_ref, acc_ref, peak_ref, total_ref, gq_ref, gk_ref,
    q_send, q_recv, kv_send, kv_recv, kv_relay, local_sem, st_send, st_recv,
    g_send, g_relay, g_recv, sq_send, sq_recv,
):
    blocks, length, width = qt_ref.shape
    planes = kvt_ref.shape[0]
    group = blocks // planes
    me, side = lax.axis_index("ctx"), lax.axis_index("head")
    plane, spot = me // group, me % group
    features = w_ref.shape[1] // 2
    rows = 2 * length
    steps = blocks // 2

    barrier = pltpu.get_barrier_semaphore()

    def greet(t):
        @pl.when(t != me)
        def _():
            pl.semaphore_signal(
                barrier, inc=1, device_id={"ctx": t}, device_id_type=pl.DeviceIdType.MESH
            )

    each(blocks, greet)
    pl.semaphore_signal(
        barrier, inc=1, device_id={"head": 1 - side}, device_id_type=pl.DeviceIdType.MESH
    )
    pl.semaphore_wait(barrier, blocks)

    def kv_column(g):
        return remote(
            kvt_ref.at[g], kv_all.at[me], kv_send.at[g], kv_recv.at[me], ctx=g * group + spot
        )

    def kv_own(r):
        return remote(
            kvt_ref.at[plane], kv_all.at[me], kv_relay.at[plane, r], kv_recv.at[me],
            ctx=plane * group + r,
        )

    def kv_pass(z, r):
        block = z * group + spot
        return remote(
            kv_all.at[block], kv_all.at[block], kv_relay.at[z, r], kv_recv.at[block],
            ctx=plane * group + r,
        )

    def q_copy(t):
        return remote(qt_ref.at[t], q_all.at[me], q_send.at[t], q_recv.at[me], ctx=t)

    def q_arrival(b):
        return remote(qt_ref.at[b], q_all.at[b], q_send.at[b], q_recv.at[b], ctx=b)

    def kv_arrival(b):
        return remote(
            kv_all.at[b], kv_all.at[b], kv_send.at[0], kv_recv.at[b], ctx=b
        )

    def st_copy(b):
        return remote(mix_ref.at[b], student_ref.at[me], st_send.at[b], st_recv.at[me], ctx=b)

    def st_arrival(b):
        return remote(mix_ref.at[b], student_ref.at[b], st_send.at[b], st_recv.at[b], ctx=b)

    def g_column(part, z):
        piece = gat_ref.at[me, part]
        return remote(
            piece, piece, g_send.at[part, z], g_recv.at[me, part], ctx=z * group + spot
        )

    def g_pass(part, z, r):
        block = z * group + spot
        piece = gat_ref.at[block, part]
        return remote(
            piece, piece, g_relay.at[part, z, r], g_recv.at[block, part], ctx=plane * group + r
        )

    def g_arrival(part, b):
        piece = gat_ref.at[b, part]
        return remote(piece, piece, g_send.at[part, 0], g_recv.at[b, part], ctx=b)

    def planes_but_mine(body):
        def one(z):
            @pl.when(z != plane)
            def _():
                body(z)

        each(planes, one)

    def spots_but_mine(body):
        def one(r):
            @pl.when(r != spot)
            def _():
                body(r)

        each(group, one)

    planes_but_mine(lambda g: kv_column(g).start())
    spots_but_mine(lambda r: kv_own(r).start())
    own_kv = pltpu.make_async_copy(kvt_ref.at[plane], kv_all.at[me], local_sem.at[0])
    own_q = pltpu.make_async_copy(qt_ref.at[me], q_all.at[me], local_sem.at[1])
    own_kv.start()
    own_q.start()
    each(blocks - 1, lambda d: q_copy((me + d + 1) % blocks).start())
    scale = 1.0 / math.sqrt(width)
    lane = lax.broadcasted_iota(jnp.int32, (rows, 2 * features), 1)
    is_upper = lane < features
    row_half = lax.broadcasted_iota(jnp.int32, (2 * features, 2 * features), 0) < features
    col_half = lax.broadcasted_iota(jnp.int32, (2 * features, 2 * features), 1) < features
    halves = jnp.where(row_half == col_half, 1.0, 0.0).astype(bf16)
    w = w_ref[...]
    wq, wk = w[:, :features], w[:, features:]
    wq_ref[...] = cat(split(cat([wq, -wq], 1), 3), 0)
    wk_ref[...] = cat(split(cat([wk, -wk], 1), 3), 0)
    for ref in (state_ref, norm_ref, last_ref, lastn_ref, gq_ref, gk_ref):
        ref[...] = jnp.zeros_like(ref)
    own_kv.wait()
    own_q.wait()

    def pass_on(z):
        kv_arrival(z * group + spot).wait_recv()
        spots_but_mine(lambda r: kv_pass(z, r).start())

    planes_but_mine(pass_on)

    def load(part, i):
        if part == 0:
            return q_all[pl.ds(2 * i, 2)].reshape(rows, width)
        return kv_all[pl.ds(2 * i, 2), part - 1].reshape(rows, width)

    def arrived(b):
        @pl.when(b != me)
        def _():
            q_arrival(b).wait_recv()

        @pl.when(b % group != spot)
        def _():
            kv_arrival(b).wait_recv()

    def send_student(b):
        @pl.when(b != me)
        def _():
            st_copy(b).start()

        @pl.when(b == me)
        def _():
            student_ref[me] = mix_ref[me]

    def send_grad(part):
        planes_but_mine(lambda z: g_column(part, z).start())
        spots_but_mine(lambda r: g_pass(part, plane, r).start())

    def relay_grad(part):
        def one(z):
            g_arrival(part, z * group + spot).wait_recv()
            spots_but_mine(lambda r: g_pass(part, z, r).start())

        planes_but_mine(one)

    def forward(i, carry):
        arrived(2 * i)
        arrived(2 * i + 1)
        q, k, v = load(0, i), load(1, i), load(2, i)
        acc_ref[...] = jnp.zeros_like(acc_ref)
        total_ref[...] = jnp.zeros_like(total_ref)
        peak_ref[...] = jnp.full(peak_ref.shape, big_negative, f32)

        def score(j, carry):
            s = mxu(q, load(1, j), NT) * scale
            score_ref[j] = s
            peak_ref[...] = jnp.maximum(
                peak_ref[...], jnp.maximum(s[:, :length], s[:, length:])
            )
            return carry

        lax.fori_loop(0, i, score, 0)
        s = mxu(q, k, NT) * scale
        causal = lax.broadcasted_iota(jnp.int32, (rows, rows), 1) <= lax.broadcasted_iota(
            jnp.int32, (rows, rows), 0
        )
        s = jnp.where(causal, s, big_negative)
        score_ref[i] = s
        row_max = jnp.max(
            jnp.maximum(peak_ref[...], jnp.maximum(s[:, :length], s[:, length:])),
            axis=-1,
            keepdims=True,
        )

        def weigh(j, carry):
            p = jnp.exp(score_ref[j] - row_max)
            total_ref[...] += p[:, :length] + p[:, length:]
            acc_ref[...] += mxu(p.astype(bf16), load(2, j), NN)
            return carry

        lax.fori_loop(0, i + 1, weigh, 0)
        teacher = acc_ref[...] / jnp.sum(total_ref[...], axis=-1, keepdims=True)

        before = jnp.maximum(i - 1, 0)
        prev_top = score_ref[before, :length, length:]
        prev_top = jnp.where(i > 0, prev_top, big_negative)
        prev = cat([prev_top, s[length:, :length]], 0)
        own = cat([s[:length, :length], s[length:, length:]], 0)
        win_max = jnp.max(jnp.maximum(prev, own), axis=-1, keepdims=True)
        p_prev, p_own = jnp.exp(prev - win_max), jnp.exp(own - win_max)
        win_den = jnp.sum(p_prev + p_own, axis=-1, keepdims=True)
        b_prev, b_own = p_prev.astype(bf16), p_own.astype(bf16)
        v_before = kv_all[jnp.maximum(2 * i - 1, 0), 1]
        win_num = cat(
            [
                mxu(cat([b_prev[:length], b_own[:length]], 1), cat([v_before, v[:length]], 0), NN),
                mxu(cat([b_prev[length:], b_own[length:]], 1), v, NN),
            ],
            0,
        )

        qf = half_softmax(mxu(cat([q, q, q], 1), wq_ref[...], NN), is_upper, halves)
        kf = half_softmax(mxu(cat([k, k, k], 1), wk_ref[...], NN), is_upper, halves)
        kfeat_ref[i] = kf
        own_0 = wide_by_exact(kf[:length], v[:length], TN)
        own_1 = wide_by_exact(kf[length:], v[length:], TN)
        sum_0 = jnp.sum(kf[:length], axis=0, keepdims=True)
        sum_1 = jnp.sum(kf[length:], axis=0, keepdims=True)
        state_0, norm_0 = state_ref[...], norm_ref[...]
        state_1, norm_1 = state_0 + last_ref[...], norm_0 + lastn_ref[...]
        state_ref[...], norm_ref[...] = state_1 + own_0, norm_1 + sum_0
        last_ref[...], lastn_ref[...] = own_1, sum_1

        norm = cat(
            [
                jnp.broadcast_to(norm_0, (length, 2 * features)),
                jnp.broadcast_to(norm_1, (length, 2 * features)),
            ],
            0,
        )
        decay = jnp.exp(-win_max)
        far = cat(
            [wide_by_wide(qf[:length], state_0, NN), wide_by_wide(qf[length:], state_1, NN)], 0
        )
        den = win_den + decay * jnp.sum(qf * norm, axis=-1, keepdims=True)
        mix = (win_num + decay * far) / den
        mix_ref[pl.ds(2 * i, 2)] = mix.astype(bf16).reshape(2, length, width)
        send_student(2 * i)
        send_student(2 * i + 1)
        mismatch = mix - teacher
        g_num = mismatch / den
        g_den = -jnp.sum(mismatch * mix, axis=-1, keepdims=True) / den
        lifted = decay * qf
        gstate_ref[2 * i] = wide_by_wide(lifted[:length], g_num[:length], TN)
        gstate_ref[2 * i + 1] = wide_by_wide(lifted[length:], g_num[length:], TN)
        pulled_norm = lifted * g_den
        gnorm_ref[2 * i] = jnp.sum(pulled_norm[:length], axis=0, keepdims=True)
        gnorm_ref[2 * i + 1] = jnp.sum(pulled_norm[length:], axis=0, keepdims=True)
        g_qf = decay * (
            cat(
                [
                    wide_by_wide(g_num[:length], state_0, NT),
                    wide_by_wide(g_num[length:], state_1, NT),
                ],
                0,
            )
            + norm * g_den
        )
        d_q = qf * (g_qf - half_sum(qf * g_qf, halves))
        gq_ref[...] += wide_by_exact(d_q, q, TN)
        return carry

    lax.fori_loop(0, steps, forward, 0)
    gat_ref[me, 0] = gq_ref[:features] - gq_ref[features:]
    send_grad(0)

    for ref in (state_ref, norm_ref):
        ref[...] = jnp.zeros_like(ref)

    def backward(step, carry):
        i = steps - 1 - step
        k, v, kf = load(1, i), load(2, i), kfeat_ref[i]
        nxt = jnp.minimum(i + 1, steps - 1)
        live = jnp.where(step > 0, 1.0, 0.0)
        later_1, later_n1 = state_ref[...], norm_ref[...]
        later_0 = later_1 + live * gstate_ref[2 * nxt]
        later_n0 = later_n1 + live * gnorm_ref[2 * nxt]
        g_kf = cat(
            [
                exact_by_wide(v[:length], later_0, NT) + later_n0,
                exact_by_wide(v[length:], later_1, NT) + later_n1,
            ],
            0,
        )
        d_k = kf * (g_kf - half_sum(kf * g_kf, halves))
        gk_ref[...] += wide_by_exact(d_k, k, TN)
        state_ref[...] = later_0 + gstate_ref[2 * i + 1]
        norm_ref[...] = later_n0 + gnorm_ref[2 * i + 1]
        return carry

    lax.fori_loop(0, steps // 2, backward, 0)
    relay_grad(0)
    lax.fori_loop(steps // 2, steps, backward, 0)
    gat_ref[me, 1] = gk_ref[:features] - gk_ref[features:]
    send_grad(1)
    relay_grad(1)

    def gathered(b):
        @pl.when(b % group != spot)
        def _():
            g_arrival(0, b).wait_recv()
            g_arrival(1, b).wait_recv()

    each(blocks, gathered)
    squares = jnp.zeros((8, width), f32)
    for b in range(blocks):
        piece = gat_ref[b].reshape(2 * features // 8, 8, width)
        squares = squares + jnp.sum(piece * piece, axis=0)
    sq_ref[0] = squares
    swap = remote(sq_ref.at[0], sq_ref.at[1], sq_send.at[0], sq_recv.at[0], head=1 - side)
    swap.start()

    def turned(b):
        update_ref[b] = gat_ref[b].reshape(2 * features, width).T

    each(blocks, turned)

    def settle(t):
        @pl.when(t != me)
        def _():
            q_copy(t).wait_send()
            st_copy(t).wait_send()
            st_arrival(t).wait_recv()

    each(blocks, settle)

    def settle_plane(z):
        @pl.when(z != plane)
        def _():
            kv_column(z).wait_send()
            g_column(0, z).wait_send()
            g_column(1, z).wait_send()

        def one(r):
            kv_pass(z, r).wait_send()
            g_pass(0, z, r).wait_send()
            g_pass(1, z, r).wait_send()

        spots_but_mine(one)

    each(planes, settle_plane)
    swap.wait()
    entries = 2 * blocks * width * 2 * features
    total = jnp.sum(sq_ref[0] + sq_ref[1], keepdims=True)
    inverse = 1.0 / jnp.sqrt(total / entries + 1e-06)

    def scaled(b):
        update_ref[b] = update_ref[b] * inverse

    each(blocks, scaled)


def whole_head(qt, kvt, w):
    blocks, length, width = qt.shape
    planes = kvt.shape[0]
    group = blocks // planes
    double = w.shape[1]
    rows, steps = 2 * length, blocks // 2
    vmem, dma = pltpu.VMEM, pltpu.SemaphoreType.DMA
    return pl.pallas_call(
        head_kernel,
        out_shape=(
            jax.ShapeDtypeStruct((blocks, length, width), bf16),
            jax.ShapeDtypeStruct((blocks, width, double), f32),
        ),
        in_specs=[pl.BlockSpec(memory_space=vmem)] * 3,
        out_specs=(pl.BlockSpec(memory_space=vmem),) * 2,
        scratch_shapes=[
            vmem((blocks, length, width), bf16),
            vmem((blocks, 2, length, width), bf16),
            vmem((blocks, length, width), bf16),
            vmem((blocks, 2, double // 2, width), f32),
            vmem((2, 8, width), f32),
            vmem((steps, rows, rows), f32),
            vmem((steps, rows, double), f32),
            vmem((blocks, double, width), f32),
            vmem((blocks, 1, double), f32),
            vmem((double, width), f32),
            vmem((1, double), f32),
            vmem((double, width), f32),
            vmem((1, double), f32),
            vmem((3 * width, double), bf16),
            vmem((3 * width, double), bf16),
            vmem((rows, width), f32),
            vmem((rows, length), f32),
            vmem((rows, length), f32),
            vmem((double, width), f32),
            vmem((double, width), f32),
            dma((blocks,)),
            dma((blocks,)),
            dma((planes,)),
            dma((blocks,)),
            dma((planes, group)),
            dma((2,)),
            dma((blocks,)),
            dma((blocks,)),
            dma((2, planes)),
            dma((2, planes, group)),
            dma((blocks, 2)),
            dma((1,)),
            dma((1,)),
        ],
        compiler_params=pltpu.CompilerParams(
            vmem_limit_bytes=40 * 2**20, collective_id=0, has_side_effects=True
        ),
    )(qt, kvt, w)


def head_shards(queries, keys, values, feature_weight):
    qt = jnp.transpose(queries, (1, 0, 2))
    kvt = jnp.transpose(jnp.stack([keys, values]), (2, 0, 1, 3))
    w = lax.dynamic_index_in_dim(feature_weight, lax.axis_index("ctx"), 0, False)
    student, update = whole_head(qt, kvt, w)
    return (jnp.transpose(student, (1, 0, 2)), update)


def shards(queries, keys, values, feature_weight):
    count = lax.axis_size("ctx")
    width = queries.shape[2]
    fits = queries.shape[1] == count and lax.axis_size("head") == 2 and count % 2 == 0 and count * queries.shape[0] <= 4096
    fits = fits and queries.shape[0] == width and feature_weight.shape[2] == width
    body = head_shards if fits else general_shards
    return body(queries, keys, values, feature_weight)


def solution(mesh):
    return jax.shard_map(
        shards,
        mesh=mesh,
        in_specs=(
            P("ctx", "head", None),
            P("ctx", "head", None),
            P("ctx", "head", None),
            P("head", None, None),
        ),
        out_specs=(P("ctx", "head", None), P("head", None, None)),
        check_vma=False,
    )
```

```python
import functools
import math

import jax
import jax.numpy as jnp
from jax import lax
from jax.experimental import pallas as pl
from jax.experimental.pallas import tpu as pltpu
from jax.sharding import PartitionSpec as P

precise = lax.Precision.HIGHEST
big_negative = -1e30


def shifted(shard, axis, by):
    devices = lax.axis_size(axis)
    pairs = [(i, i + by) for i in range(devices) if 0 <= i + by < devices]
    return lax.ppermute(shard, axis, pairs)


def carried_in(part, axis, combine, identity):
    count = lax.axis_size(axis)
    place = lax.axis_index(axis)
    ahead = count - 1 - place
    gathered = jax.tree.map(lambda a: lax.all_gather(a, axis), part)
    state = jax.tree.map(lambda a, e: jnp.zeros_like(a) + jnp.asarray(e, a.dtype), part, identity)

    def one(step, state):
        source = count - 1 - step
        return combine(
            state, jax.tree.map(lambda a: lax.dynamic_index_in_dim(a, source, 0, False), gathered)
        )

    return lax.fori_loop(0, ahead, one, state)


def feature_map(projection):
    return jnp.concatenate(
        [jax.nn.softmax(projection, axis=-1), jax.nn.softmax(-projection, axis=-1)], axis=-1
    )


def feature_pull(projection, upstream):
    half_len = upstream.shape[-1] // 2
    upper = jax.nn.softmax(projection, axis=-1)
    lower = jax.nn.softmax(-projection, axis=-1)
    grad_upper = upstream[..., :half_len]
    grad_lower = upstream[..., half_len:]
    upper_part = upper * (grad_upper - jnp.sum(upper * grad_upper, axis=-1, keepdims=True))
    lower_part = lower * (grad_lower - jnp.sum(lower * grad_lower, axis=-1, keepdims=True))
    return upper_part - lower_part


def add_pair(earlier, later):
    return (earlier[0] + later[0], earlier[1] + later[1])


def skip_block(carry_in):
    return carry_in


def general_shards(queries, keys, values, feature_weight):
    block_len, head_count, head_width = queries.shape
    kv_count = keys.shape[1]
    group_size = head_count // kv_count
    feature_len = feature_weight.shape[2] // 2
    my_block = lax.axis_index("ctx")
    score_scale = 1.0 / math.sqrt(head_width)
    grouped_q = queries.reshape(block_len, kv_count, group_size, head_width)
    maps_weight = feature_weight.reshape(kv_count, group_size, head_width, 2 * feature_len)
    query_map = maps_weight[..., :feature_len]
    key_map = maps_weight[..., feature_len:]
    query_pos = my_block * block_len + jnp.arange(block_len, dtype=jnp.int32)
    prev_start = (my_block - 1) * block_len
    last_row = my_block * block_len + block_len - 1
    initial = [
        jnp.full((kv_count, group_size, block_len), big_negative, jnp.float32),
        jnp.zeros((kv_count, group_size, block_len), jnp.float32),
        jnp.zeros((kv_count, group_size, block_len, head_width), jnp.float32),
    ]
    initial = initial + [
        jnp.zeros((kv_count, group_size, 2 * feature_len, head_width), jnp.float32),
        jnp.zeros((kv_count, group_size, 2 * feature_len), jnp.float32),
    ]
    initial = tuple(initial)
    piece_keys = lax.all_gather(keys, "ctx", axis=0, tiled=True)
    piece_values = lax.all_gather(values, "ctx", axis=0, tiled=True)
    piece_rows = piece_keys.shape[0]
    step_rows = math.gcd(piece_rows, 512)

    def attend(step_index, running):
        first_row = step_index * step_rows
        block_keys = lax.dynamic_slice_in_dim(piece_keys, step_index * step_rows, step_rows, 0)
        block_values = lax.dynamic_slice_in_dim(piece_values, step_index * step_rows, step_rows, 0)
        key_pos = first_row + jnp.arange(step_rows, dtype=jnp.int32)

        def compute(carry_in):
            row_max, running_sum, accumulated = (carry_in[0], carry_in[1], carry_in[2])
            scores = (
                jnp.einsum(
                    "tkgd,skd->kgts", grouped_q, block_keys, preferred_element_type=jnp.float32
                )
                * score_scale
            )
            allowed = key_pos[None, :] <= query_pos[:, None]
            scores = jnp.where(allowed, scores, big_negative)
            new_max = jnp.maximum(row_max, jnp.max(scores, axis=-1))
            attn_weight = jnp.where(allowed, jnp.exp(scores - new_max[..., None]), 0.0)
            factor = jnp.exp(row_max - new_max)
            running_sum = running_sum * factor + jnp.sum(attn_weight, axis=-1)
            accumulated = accumulated * factor[..., None] + jnp.einsum(
                "kgts,skd->kgtd",
                attn_weight.astype(jnp.bfloat16),
                block_values,
                preferred_element_type=jnp.float32,
            )
            result = [new_max, running_sum, accumulated] + list(carry_in[3:])
            in_state = (key_pos < prev_start).astype(jnp.float32)
            features = feature_map(
                jnp.einsum(
                    "skd,kgdf->kgsf", block_keys.astype(jnp.float32), key_map, precision=precise
                )
            )
            features = features * in_state[None, None, :, None]
            result[-2] = carry_in[-2] + jnp.einsum(
                "kgsf,skd->kgfd", features, block_values.astype(jnp.float32), precision=precise
            )
            result[-1] = carry_in[-1] + jnp.sum(features, axis=2)
            return tuple(result)

        return lax.cond(first_row <= last_row, compute, skip_block, running)

    folded = lax.fori_loop(0, piece_rows // step_rows, attend, initial)
    teacher = folded[2] / folded[1][..., None]
    stacked = jnp.stack([keys, values])
    moved = shifted(stacked, "ctx", 1)
    prev_keys, prev_values = (moved[0], moved[1])
    has_prev = (my_block > 0).astype(jnp.float32)
    window_keys = jnp.concatenate([prev_keys, keys], axis=0)
    window_values = jnp.concatenate([prev_values, values], axis=0)
    column = jnp.arange(2 * block_len, dtype=jnp.int32)
    row_index = jnp.arange(block_len, dtype=jnp.int32)
    allowed = (column[None, :] < block_len) & (my_block > 0) | (column[None, :] >= block_len) & (
        column[None, :] - block_len <= row_index[:, None]
    )
    scores = (
        jnp.einsum("tkgd,skd->kgts", grouped_q, window_keys, preferred_element_type=jnp.float32)
        * score_scale
    )
    scores = jnp.where(allowed, scores, big_negative)
    row_max = jnp.max(scores, axis=-1)
    window_weight = jnp.where(allowed, jnp.exp(scores - row_max[..., None]), 0.0)
    window_den = jnp.sum(window_weight, axis=-1)
    window_num = jnp.einsum(
        "kgts,skd->kgtd",
        window_weight.astype(jnp.bfloat16),
        window_values,
        preferred_element_type=jnp.float32,
    )
    key_proj = jnp.einsum(
        "skd,kgdf->kgsf", prev_keys.astype(jnp.float32), key_map, precision=precise
    )
    state, norm = (folded[-2], folded[-1])
    query_proj = jnp.einsum(
        "tkgd,kgdf->kgtf", grouped_q.astype(jnp.float32), query_map, precision=precise
    )
    query_feats = feature_map(query_proj)
    decay = jnp.exp(-row_max)
    far_num = decay[..., None] * jnp.einsum(
        "kgtf,kgfd->kgtd", query_feats, state, precision=precise
    )
    far_den = decay * jnp.einsum("kgtf,kgf->kgt", query_feats, norm, precision=precise)
    denominator = window_den + far_den
    mix = (window_num + far_num) / denominator[..., None]
    student = jnp.transpose(mix.astype(jnp.bfloat16), (2, 0, 1, 3)).reshape(
        block_len, head_count, head_width
    )
    mismatch = mix - teacher
    grad_num = mismatch / denominator[..., None]
    grad_den = -jnp.sum(mismatch * mix, axis=-1) / denominator
    lifted = decay[..., None] * query_feats
    grad_state = jnp.einsum("kgtf,kgtd->kgfd", lifted, grad_num, precision=precise)
    grad_norm = jnp.einsum("kgtf,kgt->kgf", lifted, grad_den, precision=precise)
    grad_qfeat = decay[..., None] * (
        jnp.einsum("kgfd,kgtd->kgtf", state, grad_num, precision=precise)
        + norm[:, :, None, :] * grad_den[..., None]
    )
    later_state, later_norm = carried_in(
        (grad_state, grad_norm),
        "ctx",
        add_pair,
        (jnp.zeros_like(grad_state), jnp.zeros_like(grad_norm)),
    )
    grad_kfeat = (
        jnp.einsum(
            "kgfd,skd->kgsf", later_state, prev_values.astype(jnp.float32), precision=precise
        )
        + later_norm[:, :, None, :]
    ) * has_prev
    grad_query = jnp.einsum(
        "tkgd,kgtf->kgdf",
        grouped_q.astype(jnp.float32),
        feature_pull(query_proj, grad_qfeat),
        precision=precise,
    )
    grad_key = jnp.einsum(
        "skd,kgsf->kgdf",
        prev_keys.astype(jnp.float32),
        feature_pull(key_proj, grad_kfeat),
        precision=precise,
    )
    gradients = jnp.concatenate([grad_query, grad_key], axis=-1).reshape(
        head_count, head_width, 2 * feature_len
    )
    entry_count = gradients.size * lax.axis_size("head")
    summed = lax.psum(gradients, "ctx")
    squares = lax.psum(jnp.sum(summed * summed), "head")
    update = summed / jnp.sqrt(squares / entry_count + 1e-06)
    return (student, update)


f32, bf16 = jnp.float32, jnp.bfloat16
NN = (((1,), (0,)), ((), ()))
NT = (((1,), (1,)), ((), ()))
TN = (((0,), (0,)), ((), ()))


def mxu(a, b, dims):
    return lax.dot_general(a, b, dims, preferred_element_type=f32)


def split(x, pieces):
    out = []
    for _ in range(pieces):
        piece = x.astype(bf16)
        out.append(piece)
        x = x - piece.astype(f32)
    return out


def cat(parts, axis):
    return jnp.concatenate(parts, axis=axis)


def exact_by_wide(a, b, dims):
    return mxu(cat([a, a], dims[0][0][0]), cat(split(b, 2), dims[0][1][0]), dims)


def wide_by_exact(a, b, dims):
    return mxu(cat(split(a, 2), dims[0][0][0]), cat([b, b], dims[0][1][0]), dims)


def wide_by_wide(a, b, dims):
    a_hi, a_lo = split(a, 2)
    b_hi, b_lo = split(b, 2)
    return mxu(
        cat([a_hi, a_hi, a_lo], dims[0][0][0]), cat([b_hi, b_lo, b_hi], dims[0][1][0]), dims
    )


def half_sum(x, halves):
    return wide_by_exact(x, halves, NN)


def half_softmax(u, is_upper, halves):
    top = jnp.max(jnp.where(is_upper, u, big_negative), axis=-1, keepdims=True)
    low = jnp.max(jnp.where(is_upper, big_negative, u), axis=-1, keepdims=True)
    e = jnp.exp(u - jnp.where(is_upper, top, low))
    return e / half_sum(e, halves)


def remote(src, dst, send_sem, recv_sem, **where):
    return pltpu.make_async_remote_copy(
        src_ref=src,
        dst_ref=dst,
        send_sem=send_sem,
        recv_sem=recv_sem,
        device_id=where,
        device_id_type=pl.DeviceIdType.MESH,
    )


def each(count, body):
    def step(index, carry):
        body(index)
        return carry

    lax.fori_loop(0, count, step, 0)


def head_kernel(
    qt_ref, kvt_ref, w_ref, student_ref, update_ref,
    q_all, kv_all, mix_ref, gat_ref, gat_key_ref, sq_ref, own_ref, sum_ref, pre_ref, pre_norm_ref,
    score_ref, kfeat_ref, gstate_ref, gnorm_ref, state_ref, norm_ref,
    wq_ref, wk_ref, acc_ref, peak_ref, total_ref, gq_ref, gk_ref,
    q_send, q_recv, kv_send, kv_recv, kv_relay, local_sem, st_send, st_recv,
    g_send, g_relay, g_recv, sq_send, sq_recv,
):
    blocks, length, width = qt_ref.shape
    planes = kvt_ref.shape[0]
    group = blocks // planes
    me, side = lax.axis_index("ctx"), lax.axis_index("head")
    plane, spot = me // group, me % group
    features = w_ref.shape[1] // 2
    rows = 2 * length
    steps = blocks // 2

    gats = (gat_ref, gat_key_ref)
    barrier = pltpu.get_barrier_semaphore()

    def greet(t):
        @pl.when(t != me)
        def _():
            pl.semaphore_signal(
                barrier, inc=1, device_id={"ctx": t}, device_id_type=pl.DeviceIdType.MESH
            )

    each(blocks, greet)
    pl.semaphore_signal(
        barrier, inc=1, device_id={"head": 1 - side}, device_id_type=pl.DeviceIdType.MESH
    )
    pl.semaphore_wait(barrier, blocks)

    def kv_column(g):
        return remote(
            kvt_ref.at[g], kv_all.at[me], kv_send.at[g], kv_recv.at[me], ctx=g * group + spot
        )

    def kv_own(r):
        return remote(
            kvt_ref.at[plane], kv_all.at[me], kv_relay.at[plane, r], kv_recv.at[me],
            ctx=plane * group + r,
        )

    def kv_pass(z, r):
        block = z * group + spot
        return remote(
            kv_all.at[block], kv_all.at[block], kv_relay.at[z, r], kv_recv.at[block],
            ctx=plane * group + r,
        )

    def q_copy(t):
        return remote(qt_ref.at[t], q_all.at[me], q_send.at[t], q_recv.at[me], ctx=t)

    def q_arrival(b):
        return remote(qt_ref.at[b], q_all.at[b], q_send.at[b], q_recv.at[b], ctx=b)

    def kv_arrival(b):
        return remote(
            kv_all.at[b], kv_all.at[b], kv_send.at[0], kv_recv.at[b], ctx=b
        )

    def st_copy(b):
        return remote(mix_ref.at[b], student_ref.at[me], st_send.at[b], st_recv.at[me], ctx=b)

    def st_arrival(b):
        return remote(mix_ref.at[b], student_ref.at[b], st_send.at[b], st_recv.at[b], ctx=b)

    def g_column(part, z):
        piece = gats[part].at[me]
        return remote(
            piece, piece, g_send.at[part, z], g_recv.at[me, part], ctx=z * group + spot
        )

    def g_pass(part, z, r):
        block = z * group + spot
        piece = gats[part].at[block]
        return remote(
            piece, piece, g_relay.at[part, z, r], g_recv.at[block, part], ctx=plane * group + r
        )

    def g_arrival(part, b):
        piece = gats[part].at[b]
        return remote(piece, piece, g_send.at[part, 0], g_recv.at[b, part], ctx=b)

    def planes_but_mine(body):
        def one(z):
            @pl.when(z != plane)
            def _():
                body(z)

        each(planes, one)

    def spots_but_mine(body):
        def one(r):
            @pl.when(r != spot)
            def _():
                body(r)

        each(group, one)

    planes_but_mine(lambda g: kv_column(g).start())
    spots_but_mine(lambda r: kv_own(r).start())
    own_kv = pltpu.make_async_copy(kvt_ref.at[plane], kv_all.at[me], local_sem.at[0])
    own_q = pltpu.make_async_copy(qt_ref.at[me], q_all.at[me], local_sem.at[1])
    own_kv.start()
    own_q.start()
    scale = 1.0 / math.sqrt(width)
    lane = lax.broadcasted_iota(jnp.int32, (rows, 2 * features), 1)
    is_upper = lane < features
    row_half = lax.broadcasted_iota(jnp.int32, (2 * features, 2 * features), 0) < features
    col_half = lax.broadcasted_iota(jnp.int32, (2 * features, 2 * features), 1) < features
    halves = jnp.where(row_half == col_half, 1.0, 0.0).astype(bf16)
    w = w_ref[...]
    wq, wk = w[:, :features], w[:, features:]
    wq_ref[...] = cat(split(cat([wq, -wq], 1), 3), 0)
    wk_ref[...] = cat(split(cat([wk, -wk], 1), 3), 0)
    for ref in (state_ref, norm_ref, gq_ref, gk_ref):
        ref[...] = jnp.zeros_like(ref)
    own_kv.wait()
    own_q.wait()

    def pass_on(z):
        kv_arrival(z * group + spot).wait_recv()
        spots_but_mine(lambda r: kv_pass(z, r).start())


    def load(part, i):
        if part == 0:
            return q_all[pl.ds(2 * i, 2)].reshape(rows, width)
        return kv_all[pl.ds(2 * i, 2), part - 1].reshape(rows, width)

    def q_arrived(b):
        @pl.when(b != me)
        def _():
            q_arrival(b).wait_recv()

    def kv_arrived(b):
        @pl.when(b % group != spot)
        def _():
            kv_arrival(b).wait_recv()

    def send_student(b):
        @pl.when(b != me)
        def _():
            st_copy(b).start()

        @pl.when(b == me)
        def _():
            student_ref[me] = mix_ref[me]

    def send_grad(part):
        planes_but_mine(lambda z: g_column(part, z).start())
        spots_but_mine(lambda r: g_pass(part, plane, r).start())

    def relay_grad(part):
        def one(z):
            g_arrival(part, z * group + spot).wait_recv()
            spots_but_mine(lambda r: g_pass(part, z, r).start())

        planes_but_mine(one)

    def key_side(i):
        kv_arrived(2 * i)
        kv_arrived(2 * i + 1)
        k, v = load(1, i), load(2, i)
        kf = half_softmax(mxu(cat([k, k, k], 1), wk_ref[...], NN), is_upper, halves)
        kfeat_ref[i] = kf
        own_ref[2 * i] = wide_by_exact(kf[:length], v[:length], TN)
        own_ref[2 * i + 1] = wide_by_exact(kf[length:], v[length:], TN)
        sum_ref[2 * i] = jnp.sum(kf[:length], axis=0, keepdims=True)
        sum_ref[2 * i + 1] = jnp.sum(kf[length:], axis=0, keepdims=True)

    def stage(dz):
        @pl.when(dz < planes - 1)
        def _():
            pass_on((plane + dz + 1) % planes)

        def push(u):
            d = dz * group + u

            @pl.when(d > 0)
            def _():
                q_copy((me + blocks - d) % blocks).start()

        each(group, push)
        half = group // 2
        each(half, lambda u: key_side((plane + dz) % planes * half + u))

    each(planes, stage)
    for b in range(2):
        pre_ref[b] = jnp.zeros_like(pre_ref[b])
        pre_norm_ref[b] = jnp.zeros_like(pre_norm_ref[b])

    def prefix(b):
        pre_ref[b + 2] = pre_ref[b + 1] + own_ref[b]
        pre_norm_ref[b + 2] = pre_norm_ref[b + 1] + sum_ref[b]

    each(blocks - 2, prefix)

    def forward(turn, carry):
        i = (me // 2 + turn) % steps
        q_arrived(2 * i)
        q_arrived(2 * i + 1)
        q, v = load(0, i), load(2, i)
        acc_ref[...] = jnp.zeros_like(acc_ref)
        total_ref[...] = jnp.zeros_like(total_ref)
        peak_ref[...] = jnp.full(peak_ref.shape, big_negative, f32)

        def pair_of(part, j):
            return cat([load(part, 2 * j), load(part, 2 * j + 1)], 0)

        def keep(j, s):
            score_ref[2 * j] = s[:, :rows]
            score_ref[2 * j + 1] = s[:, rows:]
            top = jnp.maximum(s[:, :rows], s[:, rows:])
            peak_ref[...] = jnp.maximum(
                peak_ref[...], jnp.maximum(top[:, :length], top[:, length:])
            )

        last = i // 2
        each(last, lambda j: keep(j, mxu(q, pair_of(1, j), NT) * scale))
        s = mxu(q, pair_of(1, last), NT) * scale
        column = lax.broadcasted_iota(jnp.int32, (rows, 2 * rows), 1)
        row = lax.broadcasted_iota(jnp.int32, (rows, 2 * rows), 0)
        keep(last, jnp.where(column <= row + (i - 2 * last) * rows, s, big_negative))
        row_max = jnp.max(peak_ref[...], axis=-1, keepdims=True)

        def weigh(j):
            p0 = jnp.exp(score_ref[2 * j] - row_max)
            p1 = jnp.exp(score_ref[2 * j + 1] - row_max)
            both = p0 + p1
            total_ref[...] += both[:, :length] + both[:, length:]
            p = cat([p0.astype(bf16), p1.astype(bf16)], 1)
            acc_ref[...] += mxu(p, pair_of(2, j), NN)

        each(last + 1, weigh)
        teacher = acc_ref[...] / jnp.sum(total_ref[...], axis=-1, keepdims=True)

        before = jnp.maximum(i - 1, 0)
        s = score_ref[i]
        prev_top = score_ref[before, :length, length:]
        prev_top = jnp.where(i > 0, prev_top, big_negative)
        prev = cat([prev_top, s[length:, :length]], 0)
        own = cat([s[:length, :length], s[length:, length:]], 0)
        win_max = jnp.max(jnp.maximum(prev, own), axis=-1, keepdims=True)
        p_prev, p_own = jnp.exp(prev - win_max), jnp.exp(own - win_max)
        win_den = jnp.sum(p_prev + p_own, axis=-1, keepdims=True)
        b_prev, b_own = p_prev.astype(bf16), p_own.astype(bf16)
        v_before = kv_all[jnp.maximum(2 * i - 1, 0), 1]
        win_num = cat(
            [
                mxu(cat([b_prev[:length], b_own[:length]], 1), cat([v_before, v[:length]], 0), NN),
                mxu(cat([b_prev[length:], b_own[length:]], 1), v, NN),
            ],
            0,
        )

        qf = half_softmax(mxu(cat([q, q, q], 1), wq_ref[...], NN), is_upper, halves)
        state_0, norm_0 = pre_ref[2 * i], pre_norm_ref[2 * i]
        state_1, norm_1 = pre_ref[2 * i + 1], pre_norm_ref[2 * i + 1]

        norm = cat(
            [
                jnp.broadcast_to(norm_0, (length, 2 * features)),
                jnp.broadcast_to(norm_1, (length, 2 * features)),
            ],
            0,
        )
        decay = jnp.exp(-win_max)
        far = cat(
            [wide_by_wide(qf[:length], state_0, NN), wide_by_wide(qf[length:], state_1, NN)], 0
        )
        den = win_den + decay * jnp.sum(qf * norm, axis=-1, keepdims=True)
        mix = (win_num + decay * far) / den
        mix_ref[pl.ds(2 * i, 2)] = mix.astype(bf16).reshape(2, length, width)
        send_student(2 * i)
        send_student(2 * i + 1)
        mismatch = mix - teacher
        g_num = mismatch / den
        g_den = -jnp.sum(mismatch * mix, axis=-1, keepdims=True) / den
        lifted = decay * qf
        gstate_ref[2 * i] = wide_by_wide(lifted[:length], g_num[:length], TN)
        gstate_ref[2 * i + 1] = wide_by_wide(lifted[length:], g_num[length:], TN)
        pulled_norm = lifted * g_den
        gnorm_ref[2 * i] = jnp.sum(pulled_norm[:length], axis=0, keepdims=True)
        gnorm_ref[2 * i + 1] = jnp.sum(pulled_norm[length:], axis=0, keepdims=True)
        g_qf = decay * (
            cat(
                [
                    wide_by_wide(g_num[:length], state_0, NT),
                    wide_by_wide(g_num[length:], state_1, NT),
                ],
                0,
            )
            + norm * g_den
        )
        d_q = qf * (g_qf - half_sum(qf * g_qf, halves))
        gq_ref[...] += wide_by_exact(d_q, q, TN)
        return carry

    lax.fori_loop(0, steps, forward, 0)
    gat_ref[me] = gq_ref[:features] - gq_ref[features:]
    send_grad(0)

    for ref in (state_ref, norm_ref):
        ref[...] = jnp.zeros_like(ref)

    def backward(step, carry):
        i = steps - 1 - step
        k, v, kf = load(1, i), load(2, i), kfeat_ref[i]
        nxt = jnp.minimum(i + 1, steps - 1)
        live = jnp.where(step > 0, 1.0, 0.0)
        later_1, later_n1 = state_ref[...], norm_ref[...]
        later_0 = later_1 + live * gstate_ref[2 * nxt]
        later_n0 = later_n1 + live * gnorm_ref[2 * nxt]
        g_kf = cat(
            [
                exact_by_wide(v[:length], later_0, NT) + later_n0,
                exact_by_wide(v[length:], later_1, NT) + later_n1,
            ],
            0,
        )
        d_k = kf * (g_kf - half_sum(kf * g_kf, halves))
        gk_ref[...] += wide_by_exact(d_k, k, TN)
        state_ref[...] = later_0 + gstate_ref[2 * i + 1]
        norm_ref[...] = later_n0 + gnorm_ref[2 * i + 1]
        return carry

    lax.fori_loop(0, steps // 2, backward, 0)
    relay_grad(0)
    lax.fori_loop(steps // 2, steps, backward, 0)
    gat_key_ref[me] = (gk_ref[:features] - gk_ref[features:]).astype(bf16)
    send_grad(1)
    relay_grad(1)

    def gathered(b):
        @pl.when(b % group != spot)
        def _():
            g_arrival(0, b).wait_recv()
            g_arrival(1, b).wait_recv()

    each(blocks, gathered)
    squares = jnp.zeros((8, width), f32)
    for b in range(blocks):
        piece = cat([gat_ref[b], gat_key_ref[b].astype(f32)], 0)
        piece = piece.reshape(2 * features // 8, 8, width)
        squares = squares + jnp.sum(piece * piece, axis=0)
    sq_ref[0] = squares
    swap = remote(sq_ref.at[0], sq_ref.at[1], sq_send.at[0], sq_recv.at[0], head=1 - side)
    swap.start()

    def turned(b):
        update_ref[b] = cat([gat_ref[b], gat_key_ref[b].astype(f32)], 0).T

    each(blocks, turned)

    def settle(t):
        @pl.when(t != me)
        def _():
            q_copy(t).wait_send()
            st_copy(t).wait_send()
            st_arrival(t).wait_recv()

    each(blocks, settle)

    def settle_plane(z):
        @pl.when(z != plane)
        def _():
            kv_column(z).wait_send()
            g_column(0, z).wait_send()
            g_column(1, z).wait_send()

        def one(r):
            kv_pass(z, r).wait_send()
            g_pass(0, z, r).wait_send()
            g_pass(1, z, r).wait_send()

        spots_but_mine(one)

    each(planes, settle_plane)
    swap.wait()
    entries = 2 * blocks * width * 2 * features
    total = jnp.sum(sq_ref[0] + sq_ref[1], keepdims=True)
    inverse = 1.0 / jnp.sqrt(total / entries + 1e-06)

    def scaled(b):
        update_ref[b] = update_ref[b] * inverse

    each(blocks, scaled)


def whole_head(qt, kvt, w):
    blocks, length, width = qt.shape
    planes = kvt.shape[0]
    group = blocks // planes
    double = w.shape[1]
    rows, steps = 2 * length, blocks // 2
    vmem, dma = pltpu.VMEM, pltpu.SemaphoreType.DMA
    return pl.pallas_call(
        head_kernel,
        out_shape=(
            jax.ShapeDtypeStruct((blocks, length, width), bf16),
            jax.ShapeDtypeStruct((blocks, width, double), f32),
        ),
        in_specs=[pl.BlockSpec(memory_space=vmem)] * 3,
        out_specs=(pl.BlockSpec(memory_space=vmem),) * 2,
        scratch_shapes=[
            vmem((blocks, length, width), bf16),
            vmem((blocks, 2, length, width), bf16),
            vmem((blocks, length, width), bf16),
            vmem((blocks, double // 2, width), f32),
            vmem((blocks, double // 2, width), bf16),
            vmem((2, 8, width), f32),
            vmem((blocks, double, width), f32),
            vmem((blocks, 1, double), f32),
            vmem((blocks, double, width), f32),
            vmem((blocks, 1, double), f32),
            vmem((steps, rows, rows), f32),
            vmem((steps, rows, double), f32),
            vmem((blocks, double, width), f32),
            vmem((blocks, 1, double), f32),
            vmem((double, width), f32),
            vmem((1, double), f32),
            vmem((3 * width, double), bf16),
            vmem((3 * width, double), bf16),
            vmem((rows, width), f32),
            vmem((rows, length), f32),
            vmem((rows, length), f32),
            vmem((double, width), f32),
            vmem((double, width), f32),
            dma((blocks,)),
            dma((blocks,)),
            dma((planes,)),
            dma((blocks,)),
            dma((planes, group)),
            dma((2,)),
            dma((blocks,)),
            dma((blocks,)),
            dma((2, planes)),
            dma((2, planes, group)),
            dma((blocks, 2)),
            dma((1,)),
            dma((1,)),
        ],
        compiler_params=pltpu.CompilerParams(
            vmem_limit_bytes=40 * 2**20, collective_id=0, has_side_effects=True
        ),
    )(qt, kvt, w)


def head_shards(queries, keys, values, feature_weight):
    qt = jnp.transpose(queries, (1, 0, 2))
    kvt = jnp.transpose(jnp.stack([keys, values]), (2, 0, 1, 3))
    w = lax.dynamic_index_in_dim(feature_weight, lax.axis_index("ctx"), 0, False)
    student, update = whole_head(qt, kvt, w)
    return (jnp.transpose(student, (1, 0, 2)), update)


def shards(queries, keys, values, feature_weight):
    count = lax.axis_size("ctx")
    width = queries.shape[2]
    fits = queries.shape[1] == count and lax.axis_size("head") == 2 and count % 4 == 0 and count * queries.shape[0] <= 4096
    fits = fits and queries.shape[1] // keys.shape[1] % 2 == 0 and queries.shape[0] == width and feature_weight.shape[2] == width
    body = head_shards if fits else general_shards
    return body(queries, keys, values, feature_weight)


def solution(mesh):
    return jax.shard_map(
        shards,
        mesh=mesh,
        in_specs=(
            P("ctx", "head", None),
            P("ctx", "head", None),
            P("ctx", "head", None),
            P("head", None, None),
        ),
        out_specs=(P("ctx", "head", None), P("head", None, None)),
        check_vma=False,
    )
```

```python
import functools
import math

import jax
import jax.numpy as jnp
from jax import lax
from jax.experimental import pallas as pl
from jax.experimental.pallas import tpu as pltpu
from jax.sharding import PartitionSpec as P

precise = lax.Precision.HIGHEST
big_negative = -1e30


def shifted(shard, axis, by):
    devices = lax.axis_size(axis)
    pairs = [(i, i + by) for i in range(devices) if 0 <= i + by < devices]
    return lax.ppermute(shard, axis, pairs)


def carried_in(part, axis, combine, identity):
    count = lax.axis_size(axis)
    place = lax.axis_index(axis)
    ahead = count - 1 - place
    gathered = jax.tree.map(lambda a: lax.all_gather(a, axis), part)
    state = jax.tree.map(lambda a, e: jnp.zeros_like(a) + jnp.asarray(e, a.dtype), part, identity)

    def one(step, state):
        source = count - 1 - step
        return combine(
            state, jax.tree.map(lambda a: lax.dynamic_index_in_dim(a, source, 0, False), gathered)
        )

    return lax.fori_loop(0, ahead, one, state)


def feature_map(projection):
    return jnp.concatenate(
        [jax.nn.softmax(projection, axis=-1), jax.nn.softmax(-projection, axis=-1)], axis=-1
    )


def feature_pull(projection, upstream):
    half_len = upstream.shape[-1] // 2
    upper = jax.nn.softmax(projection, axis=-1)
    lower = jax.nn.softmax(-projection, axis=-1)
    grad_upper = upstream[..., :half_len]
    grad_lower = upstream[..., half_len:]
    upper_part = upper * (grad_upper - jnp.sum(upper * grad_upper, axis=-1, keepdims=True))
    lower_part = lower * (grad_lower - jnp.sum(lower * grad_lower, axis=-1, keepdims=True))
    return upper_part - lower_part


def add_pair(earlier, later):
    return (earlier[0] + later[0], earlier[1] + later[1])


def skip_block(carry_in):
    return carry_in


def general_shards(queries, keys, values, feature_weight):
    block_len, head_count, head_width = queries.shape
    kv_count = keys.shape[1]
    group_size = head_count // kv_count
    feature_len = feature_weight.shape[2] // 2
    my_block = lax.axis_index("ctx")
    score_scale = 1.0 / math.sqrt(head_width)
    grouped_q = queries.reshape(block_len, kv_count, group_size, head_width)
    maps_weight = feature_weight.reshape(kv_count, group_size, head_width, 2 * feature_len)
    query_map = maps_weight[..., :feature_len]
    key_map = maps_weight[..., feature_len:]
    query_pos = my_block * block_len + jnp.arange(block_len, dtype=jnp.int32)
    prev_start = (my_block - 1) * block_len
    last_row = my_block * block_len + block_len - 1
    initial = [
        jnp.full((kv_count, group_size, block_len), big_negative, jnp.float32),
        jnp.zeros((kv_count, group_size, block_len), jnp.float32),
        jnp.zeros((kv_count, group_size, block_len, head_width), jnp.float32),
    ]
    initial = initial + [
        jnp.zeros((kv_count, group_size, 2 * feature_len, head_width), jnp.float32),
        jnp.zeros((kv_count, group_size, 2 * feature_len), jnp.float32),
    ]
    initial = tuple(initial)
    piece_keys = lax.all_gather(keys, "ctx", axis=0, tiled=True)
    piece_values = lax.all_gather(values, "ctx", axis=0, tiled=True)
    piece_rows = piece_keys.shape[0]
    step_rows = math.gcd(piece_rows, 512)

    def attend(step_index, running):
        first_row = step_index * step_rows
        block_keys = lax.dynamic_slice_in_dim(piece_keys, step_index * step_rows, step_rows, 0)
        block_values = lax.dynamic_slice_in_dim(piece_values, step_index * step_rows, step_rows, 0)
        key_pos = first_row + jnp.arange(step_rows, dtype=jnp.int32)

        def compute(carry_in):
            row_max, running_sum, accumulated = (carry_in[0], carry_in[1], carry_in[2])
            scores = (
                jnp.einsum(
                    "tkgd,skd->kgts", grouped_q, block_keys, preferred_element_type=jnp.float32
                )
                * score_scale
            )
            allowed = key_pos[None, :] <= query_pos[:, None]
            scores = jnp.where(allowed, scores, big_negative)
            new_max = jnp.maximum(row_max, jnp.max(scores, axis=-1))
            attn_weight = jnp.where(allowed, jnp.exp(scores - new_max[..., None]), 0.0)
            factor = jnp.exp(row_max - new_max)
            running_sum = running_sum * factor + jnp.sum(attn_weight, axis=-1)
            accumulated = accumulated * factor[..., None] + jnp.einsum(
                "kgts,skd->kgtd",
                attn_weight.astype(jnp.bfloat16),
                block_values,
                preferred_element_type=jnp.float32,
            )
            result = [new_max, running_sum, accumulated] + list(carry_in[3:])
            in_state = (key_pos < prev_start).astype(jnp.float32)
            features = feature_map(
                jnp.einsum(
                    "skd,kgdf->kgsf", block_keys.astype(jnp.float32), key_map, precision=precise
                )
            )
            features = features * in_state[None, None, :, None]
            result[-2] = carry_in[-2] + jnp.einsum(
                "kgsf,skd->kgfd", features, block_values.astype(jnp.float32), precision=precise
            )
            result[-1] = carry_in[-1] + jnp.sum(features, axis=2)
            return tuple(result)

        return lax.cond(first_row <= last_row, compute, skip_block, running)

    folded = lax.fori_loop(0, piece_rows // step_rows, attend, initial)
    teacher = folded[2] / folded[1][..., None]
    stacked = jnp.stack([keys, values])
    moved = shifted(stacked, "ctx", 1)
    prev_keys, prev_values = (moved[0], moved[1])
    has_prev = (my_block > 0).astype(jnp.float32)
    window_keys = jnp.concatenate([prev_keys, keys], axis=0)
    window_values = jnp.concatenate([prev_values, values], axis=0)
    column = jnp.arange(2 * block_len, dtype=jnp.int32)
    row_index = jnp.arange(block_len, dtype=jnp.int32)
    allowed = (column[None, :] < block_len) & (my_block > 0) | (column[None, :] >= block_len) & (
        column[None, :] - block_len <= row_index[:, None]
    )
    scores = (
        jnp.einsum("tkgd,skd->kgts", grouped_q, window_keys, preferred_element_type=jnp.float32)
        * score_scale
    )
    scores = jnp.where(allowed, scores, big_negative)
    row_max = jnp.max(scores, axis=-1)
    window_weight = jnp.where(allowed, jnp.exp(scores - row_max[..., None]), 0.0)
    window_den = jnp.sum(window_weight, axis=-1)
    window_num = jnp.einsum(
        "kgts,skd->kgtd",
        window_weight.astype(jnp.bfloat16),
        window_values,
        preferred_element_type=jnp.float32,
    )
    key_proj = jnp.einsum(
        "skd,kgdf->kgsf", prev_keys.astype(jnp.float32), key_map, precision=precise
    )
    state, norm = (folded[-2], folded[-1])
    query_proj = jnp.einsum(
        "tkgd,kgdf->kgtf", grouped_q.astype(jnp.float32), query_map, precision=precise
    )
    query_feats = feature_map(query_proj)
    decay = jnp.exp(-row_max)
    far_num = decay[..., None] * jnp.einsum(
        "kgtf,kgfd->kgtd", query_feats, state, precision=precise
    )
    far_den = decay * jnp.einsum("kgtf,kgf->kgt", query_feats, norm, precision=precise)
    denominator = window_den + far_den
    mix = (window_num + far_num) / denominator[..., None]
    student = jnp.transpose(mix.astype(jnp.bfloat16), (2, 0, 1, 3)).reshape(
        block_len, head_count, head_width
    )
    mismatch = mix - teacher
    grad_num = mismatch / denominator[..., None]
    grad_den = -jnp.sum(mismatch * mix, axis=-1) / denominator
    lifted = decay[..., None] * query_feats
    grad_state = jnp.einsum("kgtf,kgtd->kgfd", lifted, grad_num, precision=precise)
    grad_norm = jnp.einsum("kgtf,kgt->kgf", lifted, grad_den, precision=precise)
    grad_qfeat = decay[..., None] * (
        jnp.einsum("kgfd,kgtd->kgtf", state, grad_num, precision=precise)
        + norm[:, :, None, :] * grad_den[..., None]
    )
    later_state, later_norm = carried_in(
        (grad_state, grad_norm),
        "ctx",
        add_pair,
        (jnp.zeros_like(grad_state), jnp.zeros_like(grad_norm)),
    )
    grad_kfeat = (
        jnp.einsum(
            "kgfd,skd->kgsf", later_state, prev_values.astype(jnp.float32), precision=precise
        )
        + later_norm[:, :, None, :]
    ) * has_prev
    grad_query = jnp.einsum(
        "tkgd,kgtf->kgdf",
        grouped_q.astype(jnp.float32),
        feature_pull(query_proj, grad_qfeat),
        precision=precise,
    )
    grad_key = jnp.einsum(
        "skd,kgsf->kgdf",
        prev_keys.astype(jnp.float32),
        feature_pull(key_proj, grad_kfeat),
        precision=precise,
    )
    gradients = jnp.concatenate([grad_query, grad_key], axis=-1).reshape(
        head_count, head_width, 2 * feature_len
    )
    entry_count = gradients.size * lax.axis_size("head")
    summed = lax.psum(gradients, "ctx")
    squares = lax.psum(jnp.sum(summed * summed), "head")
    update = summed / jnp.sqrt(squares / entry_count + 1e-06)
    return (student, update)


f32, bf16 = jnp.float32, jnp.bfloat16
NN = (((1,), (0,)), ((), ()))
NT = (((1,), (1,)), ((), ()))
TN = (((0,), (0,)), ((), ()))


def mxu(a, b, dims):
    return lax.dot_general(a, b, dims, preferred_element_type=f32)


def split(x, pieces):
    out = []
    for _ in range(pieces):
        piece = x.astype(bf16)
        out.append(piece)
        x = x - piece.astype(f32)
    return out


def cat(parts, axis):
    return jnp.concatenate(parts, axis=axis)


def exact_by_wide(a, b, dims):
    return mxu(cat([a, a], dims[0][0][0]), cat(split(b, 2), dims[0][1][0]), dims)


def wide_by_exact(a, b, dims):
    return mxu(cat(split(a, 2), dims[0][0][0]), cat([b, b], dims[0][1][0]), dims)


def wide_by_wide(a, b, dims):
    a_hi, a_lo = split(a, 2)
    b_hi, b_lo = split(b, 2)
    return mxu(
        cat([a_hi, a_hi, a_lo], dims[0][0][0]), cat([b_hi, b_lo, b_hi], dims[0][1][0]), dims
    )


def half_sum(x, halves):
    return wide_by_exact(x, halves, NN)


def half_softmax(u, is_upper, halves):
    top = jnp.max(jnp.where(is_upper, u, big_negative), axis=-1, keepdims=True)
    low = jnp.max(jnp.where(is_upper, big_negative, u), axis=-1, keepdims=True)
    e = jnp.exp(u - jnp.where(is_upper, top, low))
    return e / half_sum(e, halves)


def remote(src, dst, send_sem, recv_sem, **where):
    return pltpu.make_async_remote_copy(
        src_ref=src,
        dst_ref=dst,
        send_sem=send_sem,
        recv_sem=recv_sem,
        device_id=where,
        device_id_type=pl.DeviceIdType.MESH,
    )


def each(count, body):
    def step(index, carry):
        body(index)
        return carry

    lax.fori_loop(0, count, step, 0)


def head_kernel(
    qt_ref, kvt_ref, w_ref, student_ref, update_ref,
    q_all, kv_all, mix_ref, gat_ref, gat_key_ref, sq_ref, own_ref, sum_ref, pre_ref, pre_norm_ref,
    score_ref, kfeat_ref, gstate_ref, gnorm_ref, state_ref, norm_ref,
    wq_ref, wk_ref, acc_ref, peak_ref, total_ref, gq_ref, gk_ref,
    q_send, q_recv, kv_send, kv_recv, kv_relay, local_sem, st_send, st_recv,
    g_send, g_relay, g_recv, sq_send, sq_recv,
):
    blocks, length, width = qt_ref.shape
    planes = kvt_ref.shape[0]
    group = blocks // planes
    me, side = lax.axis_index("ctx"), lax.axis_index("head")
    plane, spot = me // group, me % group
    features = w_ref.shape[1] // 2
    rows = 2 * length
    steps = blocks // 2

    gats = (gat_ref, gat_key_ref)
    barrier = pltpu.get_barrier_semaphore()

    def greet(t):
        @pl.when(t != me)
        def _():
            pl.semaphore_signal(
                barrier, inc=1, device_id={"ctx": t}, device_id_type=pl.DeviceIdType.MESH
            )

    each(blocks, greet)
    pl.semaphore_signal(
        barrier, inc=1, device_id={"head": 1 - side}, device_id_type=pl.DeviceIdType.MESH
    )
    pl.semaphore_wait(barrier, blocks)

    def kv_column(g):
        return remote(
            kvt_ref.at[g], kv_all.at[me], kv_send.at[g], kv_recv.at[me], ctx=g * group + spot
        )

    def kv_own(r):
        return remote(
            kvt_ref.at[plane], kv_all.at[me], kv_relay.at[plane, r], kv_recv.at[me],
            ctx=plane * group + r,
        )

    def kv_pass(z, r):
        block = z * group + spot
        return remote(
            kv_all.at[block], kv_all.at[block], kv_relay.at[z, r], kv_recv.at[block],
            ctx=plane * group + r,
        )

    def q_copy(t):
        return remote(qt_ref.at[t], q_all.at[me], q_send.at[t], q_recv.at[me], ctx=t)

    def q_arrival(b):
        return remote(qt_ref.at[b], q_all.at[b], q_send.at[b], q_recv.at[b], ctx=b)

    def kv_arrival(b):
        return remote(
            kv_all.at[b], kv_all.at[b], kv_send.at[0], kv_recv.at[b], ctx=b
        )

    def st_copy(b):
        return remote(mix_ref.at[b], student_ref.at[me], st_send.at[b], st_recv.at[me], ctx=b)

    def st_arrival(b):
        return remote(mix_ref.at[b], student_ref.at[b], st_send.at[b], st_recv.at[b], ctx=b)

    def g_column(part, z):
        piece = gats[part].at[me]
        return remote(
            piece, piece, g_send.at[part, z], g_recv.at[me, part], ctx=z * group + spot
        )

    def g_pass(part, z, r):
        block = z * group + spot
        piece = gats[part].at[block]
        return remote(
            piece, piece, g_relay.at[part, z, r], g_recv.at[block, part], ctx=plane * group + r
        )

    def g_arrival(part, b):
        piece = gats[part].at[b]
        return remote(piece, piece, g_send.at[part, 0], g_recv.at[b, part], ctx=b)

    def planes_but_mine(body):
        def one(z):
            @pl.when(z != plane)
            def _():
                body(z)

        each(planes, one)

    def spots_but_mine(body):
        def one(r):
            @pl.when(r != spot)
            def _():
                body(r)

        each(group, one)

    planes_but_mine(lambda g: kv_column(g).start())
    spots_but_mine(lambda r: kv_own(r).start())
    own_kv = pltpu.make_async_copy(kvt_ref.at[plane], kv_all.at[me], local_sem.at[0])
    own_q = pltpu.make_async_copy(qt_ref.at[me], q_all.at[me], local_sem.at[1])
    own_kv.start()
    own_q.start()
    scale = 1.0 / math.sqrt(width)
    lane = lax.broadcasted_iota(jnp.int32, (rows, 2 * features), 1)
    is_upper = lane < features
    row_half = lax.broadcasted_iota(jnp.int32, (2 * features, 2 * features), 0) < features
    col_half = lax.broadcasted_iota(jnp.int32, (2 * features, 2 * features), 1) < features
    halves = jnp.where(row_half == col_half, 1.0, 0.0).astype(bf16)
    w = w_ref[...]
    wq, wk = w[:, :features], w[:, features:]
    wq_ref[...] = cat(split(cat([wq, -wq], 1), 3), 0)
    wk_ref[...] = cat(split(cat([wk, -wk], 1), 3), 0)
    for ref in (state_ref, norm_ref, gq_ref, gk_ref):
        ref[...] = jnp.zeros_like(ref)
    own_kv.wait()
    own_q.wait()

    def pass_on(z):
        kv_arrival(z * group + spot).wait_recv()
        spots_but_mine(lambda r: kv_pass(z, r).start())


    def load(part, i):
        if part == 0:
            return q_all[pl.ds(2 * i, 2)].reshape(rows, width)
        return kv_all[pl.ds(2 * i, 2), part - 1].reshape(rows, width)

    def q_arrived(b):
        @pl.when(b != me)
        def _():
            q_arrival(b).wait_recv()

    def kv_arrived(b):
        @pl.when(b % group != spot)
        def _():
            kv_arrival(b).wait_recv()

    def send_student(b):
        @pl.when(b != me)
        def _():
            st_copy(b).start()

        @pl.when(b == me)
        def _():
            student_ref[me] = mix_ref[me]

    def send_grad(part):
        planes_but_mine(lambda z: g_column(part, z).start())
        spots_but_mine(lambda r: g_pass(part, plane, r).start())

    def relay_grad(part):
        def one(z):
            g_arrival(part, z * group + spot).wait_recv()
            spots_but_mine(lambda r: g_pass(part, z, r).start())

        planes_but_mine(one)

    def key_side(i):
        kv_arrived(2 * i)
        kv_arrived(2 * i + 1)
        k, v = load(1, i), load(2, i)
        kf = half_softmax(mxu(cat([k, k, k], 1), wk_ref[...], NN), is_upper, halves)
        kfeat_ref[i] = kf
        own_ref[2 * i] = wide_by_exact(kf[:length], v[:length], TN)
        own_ref[2 * i + 1] = wide_by_exact(kf[length:], v[length:], TN)
        sum_ref[2 * i] = jnp.sum(kf[:length], axis=0, keepdims=True)
        sum_ref[2 * i + 1] = jnp.sum(kf[length:], axis=0, keepdims=True)

    def push(d):
        q_copy((me + 2 * blocks - 1 - d) % blocks).start()

    each(blocks - 1, push)

    def relay_first(dz):
        pass_on((plane + dz + 1) % planes)

    each(planes - 1, relay_first)

    def stage(dz):
        half = group // 2
        each(half, lambda u: key_side((plane + dz) % planes * half + u))

    each(planes, stage)
    for b in range(2):
        pre_ref[b] = jnp.zeros_like(pre_ref[b])
        pre_norm_ref[b] = jnp.zeros_like(pre_norm_ref[b])

    def prefix(b):
        pre_ref[b + 2] = pre_ref[b + 1] + own_ref[b]
        pre_norm_ref[b + 2] = pre_norm_ref[b + 1] + sum_ref[b]

    each(blocks - 2, prefix)

    def forward(turn, carry):
        i = (me // 2 + turn) % steps
        q_arrived(2 * i)
        q_arrived(2 * i + 1)
        q, v = load(0, i), load(2, i)
        acc_ref[...] = jnp.zeros_like(acc_ref)
        total_ref[...] = jnp.zeros_like(total_ref)
        peak_ref[...] = jnp.full(peak_ref.shape, big_negative, f32)

        def pair_of(part, j):
            return cat([load(part, 2 * j), load(part, 2 * j + 1)], 0)

        def keep(j, s):
            score_ref[2 * j] = s[:, :rows]
            score_ref[2 * j + 1] = s[:, rows:]
            top = jnp.maximum(s[:, :rows], s[:, rows:])
            peak_ref[...] = jnp.maximum(
                peak_ref[...], jnp.maximum(top[:, :length], top[:, length:])
            )

        last = i // 2
        each(last, lambda j: keep(j, mxu(q, pair_of(1, j), NT) * scale))
        s = mxu(q, pair_of(1, last), NT) * scale
        column = lax.broadcasted_iota(jnp.int32, (rows, 2 * rows), 1)
        row = lax.broadcasted_iota(jnp.int32, (rows, 2 * rows), 0)
        keep(last, jnp.where(column <= row + (i - 2 * last) * rows, s, big_negative))
        row_max = jnp.max(peak_ref[...], axis=-1, keepdims=True)

        def weigh(j):
            p0 = jnp.exp(score_ref[2 * j] - row_max)
            p1 = jnp.exp(score_ref[2 * j + 1] - row_max)
            both = p0 + p1
            total_ref[...] += both[:, :length] + both[:, length:]
            p = cat([p0.astype(bf16), p1.astype(bf16)], 1)
            acc_ref[...] += mxu(p, pair_of(2, j), NN)

        each(last + 1, weigh)
        teacher = acc_ref[...] / jnp.sum(total_ref[...], axis=-1, keepdims=True)

        before = jnp.maximum(i - 1, 0)
        s = score_ref[i]
        prev_top = score_ref[before, :length, length:]
        prev_top = jnp.where(i > 0, prev_top, big_negative)
        prev = cat([prev_top, s[length:, :length]], 0)
        own = cat([s[:length, :length], s[length:, length:]], 0)
        win_max = jnp.max(jnp.maximum(prev, own), axis=-1, keepdims=True)
        p_prev, p_own = jnp.exp(prev - win_max), jnp.exp(own - win_max)
        win_den = jnp.sum(p_prev + p_own, axis=-1, keepdims=True)
        b_prev, b_own = p_prev.astype(bf16), p_own.astype(bf16)
        v_before = kv_all[jnp.maximum(2 * i - 1, 0), 1]
        win_num = cat(
            [
                mxu(cat([b_prev[:length], b_own[:length]], 1), cat([v_before, v[:length]], 0), NN),
                mxu(cat([b_prev[length:], b_own[length:]], 1), v, NN),
            ],
            0,
        )

        qf = half_softmax(mxu(cat([q, q, q], 1), wq_ref[...], NN), is_upper, halves)
        state_0, norm_0 = pre_ref[2 * i], pre_norm_ref[2 * i]
        state_1, norm_1 = pre_ref[2 * i + 1], pre_norm_ref[2 * i + 1]

        norm = cat(
            [
                jnp.broadcast_to(norm_0, (length, 2 * features)),
                jnp.broadcast_to(norm_1, (length, 2 * features)),
            ],
            0,
        )
        decay = jnp.exp(-win_max)
        far = cat(
            [wide_by_wide(qf[:length], state_0, NN), wide_by_wide(qf[length:], state_1, NN)], 0
        )
        den = win_den + decay * jnp.sum(qf * norm, axis=-1, keepdims=True)
        mix = (win_num + decay * far) / den
        mix_ref[pl.ds(2 * i, 2)] = mix.astype(bf16).reshape(2, length, width)
        send_student(2 * i)
        send_student(2 * i + 1)
        mismatch = mix - teacher
        g_num = mismatch / den
        g_den = -jnp.sum(mismatch * mix, axis=-1, keepdims=True) / den
        lifted = decay * qf
        gstate_ref[2 * i] = wide_by_wide(lifted[:length], g_num[:length], TN)
        gstate_ref[2 * i + 1] = wide_by_wide(lifted[length:], g_num[length:], TN)
        pulled_norm = lifted * g_den
        gnorm_ref[2 * i] = jnp.sum(pulled_norm[:length], axis=0, keepdims=True)
        gnorm_ref[2 * i + 1] = jnp.sum(pulled_norm[length:], axis=0, keepdims=True)
        g_qf = decay * (
            cat(
                [
                    wide_by_wide(g_num[:length], state_0, NT),
                    wide_by_wide(g_num[length:], state_1, NT),
                ],
                0,
            )
            + norm * g_den
        )
        d_q = qf * (g_qf - half_sum(qf * g_qf, halves))
        gq_ref[...] += wide_by_exact(d_q, q, TN)
        return carry

    lax.fori_loop(0, steps, forward, 0)
    gat_ref[me] = (gq_ref[:features] - gq_ref[features:]).astype(bf16)
    send_grad(0)

    for ref in (state_ref, norm_ref):
        ref[...] = jnp.zeros_like(ref)

    def backward(step, carry):
        i = steps - 1 - step
        k, v, kf = load(1, i), load(2, i), kfeat_ref[i]
        nxt = jnp.minimum(i + 1, steps - 1)
        live = jnp.where(step > 0, 1.0, 0.0)
        later_1, later_n1 = state_ref[...], norm_ref[...]
        later_0 = later_1 + live * gstate_ref[2 * nxt]
        later_n0 = later_n1 + live * gnorm_ref[2 * nxt]
        g_kf = cat(
            [
                exact_by_wide(v[:length], later_0, NT) + later_n0,
                exact_by_wide(v[length:], later_1, NT) + later_n1,
            ],
            0,
        )
        d_k = kf * (g_kf - half_sum(kf * g_kf, halves))
        gk_ref[...] += wide_by_exact(d_k, k, TN)
        state_ref[...] = later_0 + gstate_ref[2 * i + 1]
        norm_ref[...] = later_n0 + gnorm_ref[2 * i + 1]
        return carry

    lax.fori_loop(0, steps // 2, backward, 0)
    relay_grad(0)
    lax.fori_loop(steps // 2, steps, backward, 0)
    gat_key_ref[me] = (gk_ref[:features] - gk_ref[features:]).astype(bf16)
    send_grad(1)
    relay_grad(1)

    def gathered(b):
        @pl.when(b % group != spot)
        def _():
            g_arrival(0, b).wait_recv()
            g_arrival(1, b).wait_recv()

    each(blocks, gathered)
    squares = jnp.zeros((8, width), f32)
    for b in range(blocks):
        piece = cat([gat_ref[b], gat_key_ref[b]], 0).astype(f32)
        piece = piece.reshape(2 * features // 8, 8, width)
        squares = squares + jnp.sum(piece * piece, axis=0)
    sq_ref[0] = squares
    swap = remote(sq_ref.at[0], sq_ref.at[1], sq_send.at[0], sq_recv.at[0], head=1 - side)
    swap.start()

    def turned(b):
        update_ref[b] = cat([gat_ref[b], gat_key_ref[b]], 0).astype(f32).T

    each(blocks, turned)

    def settle(t):
        @pl.when(t != me)
        def _():
            q_copy(t).wait_send()
            st_copy(t).wait_send()
            st_arrival(t).wait_recv()

    each(blocks, settle)

    def settle_plane(z):
        @pl.when(z != plane)
        def _():
            kv_column(z).wait_send()
            g_column(0, z).wait_send()
            g_column(1, z).wait_send()

        def one(r):
            kv_pass(z, r).wait_send()
            g_pass(0, z, r).wait_send()
            g_pass(1, z, r).wait_send()

        spots_but_mine(one)

    each(planes, settle_plane)
    swap.wait()
    entries = 2 * blocks * width * 2 * features
    total = jnp.sum(sq_ref[0] + sq_ref[1], keepdims=True)
    inverse = 1.0 / jnp.sqrt(total / entries + 1e-06)

    def scaled(b):
        update_ref[b] = update_ref[b] * inverse

    each(blocks, scaled)


def whole_head(qt, kvt, w):
    blocks, length, width = qt.shape
    planes = kvt.shape[0]
    group = blocks // planes
    double = w.shape[1]
    rows, steps = 2 * length, blocks // 2
    vmem, dma = pltpu.VMEM, pltpu.SemaphoreType.DMA
    return pl.pallas_call(
        head_kernel,
        out_shape=(
            jax.ShapeDtypeStruct((blocks, length, width), bf16),
            jax.ShapeDtypeStruct((blocks, width, double), f32),
        ),
        in_specs=[pl.BlockSpec(memory_space=vmem)] * 3,
        out_specs=(pl.BlockSpec(memory_space=vmem),) * 2,
        scratch_shapes=[
            vmem((blocks, length, width), bf16),
            vmem((blocks, 2, length, width), bf16),
            vmem((blocks, length, width), bf16),
            vmem((blocks, double // 2, width), bf16),
            vmem((blocks, double // 2, width), bf16),
            vmem((2, 8, width), f32),
            vmem((blocks, double, width), f32),
            vmem((blocks, 1, double), f32),
            vmem((blocks, double, width), f32),
            vmem((blocks, 1, double), f32),
            vmem((steps, rows, rows), f32),
            vmem((steps, rows, double), f32),
            vmem((blocks, double, width), f32),
            vmem((blocks, 1, double), f32),
            vmem((double, width), f32),
            vmem((1, double), f32),
            vmem((3 * width, double), bf16),
            vmem((3 * width, double), bf16),
            vmem((rows, width), f32),
            vmem((rows, length), f32),
            vmem((rows, length), f32),
            vmem((double, width), f32),
            vmem((double, width), f32),
            dma((blocks,)),
            dma((blocks,)),
            dma((planes,)),
            dma((blocks,)),
            dma((planes, group)),
            dma((2,)),
            dma((blocks,)),
            dma((blocks,)),
            dma((2, planes)),
            dma((2, planes, group)),
            dma((blocks, 2)),
            dma((1,)),
            dma((1,)),
        ],
        compiler_params=pltpu.CompilerParams(
            vmem_limit_bytes=40 * 2**20, collective_id=0, has_side_effects=True
        ),
    )(qt, kvt, w)


def head_shards(queries, keys, values, feature_weight):
    qt = jnp.transpose(queries, (1, 0, 2))
    kvt = jnp.transpose(jnp.stack([keys, values]), (2, 0, 1, 3))
    w = lax.dynamic_index_in_dim(feature_weight, lax.axis_index("ctx"), 0, False)
    student, update = whole_head(qt, kvt, w)
    return (jnp.transpose(student, (1, 0, 2)), update)


def shards(queries, keys, values, feature_weight):
    count = lax.axis_size("ctx")
    width = queries.shape[2]
    fits = queries.shape[1] == count and lax.axis_size("head") == 2 and count % 4 == 0 and count * queries.shape[0] <= 4096
    fits = fits and queries.shape[1] // keys.shape[1] % 2 == 0 and queries.shape[0] == width and feature_weight.shape[2] == width
    body = head_shards if fits else general_shards
    return body(queries, keys, values, feature_weight)


def solution(mesh):
    return jax.shard_map(
        shards,
        mesh=mesh,
        in_specs=(
            P("ctx", "head", None),
            P("ctx", "head", None),
            P("ctx", "head", None),
            P("head", None, None),
        ),
        out_specs=(P("ctx", "head", None), P("head", None, None)),
        check_vma=False,
    )
```

```python
import functools
import math

import jax
import jax.numpy as jnp
from jax import lax
from jax.experimental import pallas as pl
from jax.experimental.pallas import tpu as pltpu
from jax.sharding import PartitionSpec as P

precise = lax.Precision.HIGHEST
big_negative = -1e30


def shifted(shard, axis, by):
    devices = lax.axis_size(axis)
    pairs = [(i, i + by) for i in range(devices) if 0 <= i + by < devices]
    return lax.ppermute(shard, axis, pairs)


def carried_in(part, axis, combine, identity):
    count = lax.axis_size(axis)
    place = lax.axis_index(axis)
    ahead = count - 1 - place
    gathered = jax.tree.map(lambda a: lax.all_gather(a, axis), part)
    state = jax.tree.map(lambda a, e: jnp.zeros_like(a) + jnp.asarray(e, a.dtype), part, identity)

    def one(step, state):
        source = count - 1 - step
        return combine(
            state, jax.tree.map(lambda a: lax.dynamic_index_in_dim(a, source, 0, False), gathered)
        )

    return lax.fori_loop(0, ahead, one, state)


def feature_map(projection):
    return jnp.concatenate(
        [jax.nn.softmax(projection, axis=-1), jax.nn.softmax(-projection, axis=-1)], axis=-1
    )


def feature_pull(projection, upstream):
    half_len = upstream.shape[-1] // 2
    upper = jax.nn.softmax(projection, axis=-1)
    lower = jax.nn.softmax(-projection, axis=-1)
    grad_upper = upstream[..., :half_len]
    grad_lower = upstream[..., half_len:]
    upper_part = upper * (grad_upper - jnp.sum(upper * grad_upper, axis=-1, keepdims=True))
    lower_part = lower * (grad_lower - jnp.sum(lower * grad_lower, axis=-1, keepdims=True))
    return upper_part - lower_part


def add_pair(earlier, later):
    return (earlier[0] + later[0], earlier[1] + later[1])


def skip_block(carry_in):
    return carry_in


def general_shards(queries, keys, values, feature_weight):
    block_len, head_count, head_width = queries.shape
    kv_count = keys.shape[1]
    group_size = head_count // kv_count
    feature_len = feature_weight.shape[2] // 2
    my_block = lax.axis_index("ctx")
    score_scale = 1.0 / math.sqrt(head_width)
    grouped_q = queries.reshape(block_len, kv_count, group_size, head_width)
    maps_weight = feature_weight.reshape(kv_count, group_size, head_width, 2 * feature_len)
    query_map = maps_weight[..., :feature_len]
    key_map = maps_weight[..., feature_len:]
    query_pos = my_block * block_len + jnp.arange(block_len, dtype=jnp.int32)
    prev_start = (my_block - 1) * block_len
    last_row = my_block * block_len + block_len - 1
    initial = [
        jnp.full((kv_count, group_size, block_len), big_negative, jnp.float32),
        jnp.zeros((kv_count, group_size, block_len), jnp.float32),
        jnp.zeros((kv_count, group_size, block_len, head_width), jnp.float32),
    ]
    initial = initial + [
        jnp.zeros((kv_count, group_size, 2 * feature_len, head_width), jnp.float32),
        jnp.zeros((kv_count, group_size, 2 * feature_len), jnp.float32),
    ]
    initial = tuple(initial)
    piece_keys = lax.all_gather(keys, "ctx", axis=0, tiled=True)
    piece_values = lax.all_gather(values, "ctx", axis=0, tiled=True)
    piece_rows = piece_keys.shape[0]
    step_rows = math.gcd(piece_rows, 512)

    def attend(step_index, running):
        first_row = step_index * step_rows
        block_keys = lax.dynamic_slice_in_dim(piece_keys, step_index * step_rows, step_rows, 0)
        block_values = lax.dynamic_slice_in_dim(piece_values, step_index * step_rows, step_rows, 0)
        key_pos = first_row + jnp.arange(step_rows, dtype=jnp.int32)

        def compute(carry_in):
            row_max, running_sum, accumulated = (carry_in[0], carry_in[1], carry_in[2])
            scores = (
                jnp.einsum(
                    "tkgd,skd->kgts", grouped_q, block_keys, preferred_element_type=jnp.float32
                )
                * score_scale
            )
            allowed = key_pos[None, :] <= query_pos[:, None]
            scores = jnp.where(allowed, scores, big_negative)
            new_max = jnp.maximum(row_max, jnp.max(scores, axis=-1))
            attn_weight = jnp.where(allowed, jnp.exp(scores - new_max[..., None]), 0.0)
            factor = jnp.exp(row_max - new_max)
            running_sum = running_sum * factor + jnp.sum(attn_weight, axis=-1)
            accumulated = accumulated * factor[..., None] + jnp.einsum(
                "kgts,skd->kgtd",
                attn_weight.astype(jnp.bfloat16),
                block_values,
                preferred_element_type=jnp.float32,
            )
            result = [new_max, running_sum, accumulated] + list(carry_in[3:])
            in_state = (key_pos < prev_start).astype(jnp.float32)
            features = feature_map(
                jnp.einsum(
                    "skd,kgdf->kgsf", block_keys.astype(jnp.float32), key_map, precision=precise
                )
            )
            features = features * in_state[None, None, :, None]
            result[-2] = carry_in[-2] + jnp.einsum(
                "kgsf,skd->kgfd", features, block_values.astype(jnp.float32), precision=precise
            )
            result[-1] = carry_in[-1] + jnp.sum(features, axis=2)
            return tuple(result)

        return lax.cond(first_row <= last_row, compute, skip_block, running)

    folded = lax.fori_loop(0, piece_rows // step_rows, attend, initial)
    teacher = folded[2] / folded[1][..., None]
    stacked = jnp.stack([keys, values])
    moved = shifted(stacked, "ctx", 1)
    prev_keys, prev_values = (moved[0], moved[1])
    has_prev = (my_block > 0).astype(jnp.float32)
    window_keys = jnp.concatenate([prev_keys, keys], axis=0)
    window_values = jnp.concatenate([prev_values, values], axis=0)
    column = jnp.arange(2 * block_len, dtype=jnp.int32)
    row_index = jnp.arange(block_len, dtype=jnp.int32)
    allowed = (column[None, :] < block_len) & (my_block > 0) | (column[None, :] >= block_len) & (
        column[None, :] - block_len <= row_index[:, None]
    )
    scores = (
        jnp.einsum("tkgd,skd->kgts", grouped_q, window_keys, preferred_element_type=jnp.float32)
        * score_scale
    )
    scores = jnp.where(allowed, scores, big_negative)
    row_max = jnp.max(scores, axis=-1)
    window_weight = jnp.where(allowed, jnp.exp(scores - row_max[..., None]), 0.0)
    window_den = jnp.sum(window_weight, axis=-1)
    window_num = jnp.einsum(
        "kgts,skd->kgtd",
        window_weight.astype(jnp.bfloat16),
        window_values,
        preferred_element_type=jnp.float32,
    )
    key_proj = jnp.einsum(
        "skd,kgdf->kgsf", prev_keys.astype(jnp.float32), key_map, precision=precise
    )
    state, norm = (folded[-2], folded[-1])
    query_proj = jnp.einsum(
        "tkgd,kgdf->kgtf", grouped_q.astype(jnp.float32), query_map, precision=precise
    )
    query_feats = feature_map(query_proj)
    decay = jnp.exp(-row_max)
    far_num = decay[..., None] * jnp.einsum(
        "kgtf,kgfd->kgtd", query_feats, state, precision=precise
    )
    far_den = decay * jnp.einsum("kgtf,kgf->kgt", query_feats, norm, precision=precise)
    denominator = window_den + far_den
    mix = (window_num + far_num) / denominator[..., None]
    student = jnp.transpose(mix.astype(jnp.bfloat16), (2, 0, 1, 3)).reshape(
        block_len, head_count, head_width
    )
    mismatch = mix - teacher
    grad_num = mismatch / denominator[..., None]
    grad_den = -jnp.sum(mismatch * mix, axis=-1) / denominator
    lifted = decay[..., None] * query_feats
    grad_state = jnp.einsum("kgtf,kgtd->kgfd", lifted, grad_num, precision=precise)
    grad_norm = jnp.einsum("kgtf,kgt->kgf", lifted, grad_den, precision=precise)
    grad_qfeat = decay[..., None] * (
        jnp.einsum("kgfd,kgtd->kgtf", state, grad_num, precision=precise)
        + norm[:, :, None, :] * grad_den[..., None]
    )
    later_state, later_norm = carried_in(
        (grad_state, grad_norm),
        "ctx",
        add_pair,
        (jnp.zeros_like(grad_state), jnp.zeros_like(grad_norm)),
    )
    grad_kfeat = (
        jnp.einsum(
            "kgfd,skd->kgsf", later_state, prev_values.astype(jnp.float32), precision=precise
        )
        + later_norm[:, :, None, :]
    ) * has_prev
    grad_query = jnp.einsum(
        "tkgd,kgtf->kgdf",
        grouped_q.astype(jnp.float32),
        feature_pull(query_proj, grad_qfeat),
        precision=precise,
    )
    grad_key = jnp.einsum(
        "skd,kgsf->kgdf",
        prev_keys.astype(jnp.float32),
        feature_pull(key_proj, grad_kfeat),
        precision=precise,
    )
    gradients = jnp.concatenate([grad_query, grad_key], axis=-1).reshape(
        head_count, head_width, 2 * feature_len
    )
    entry_count = gradients.size * lax.axis_size("head")
    summed = lax.psum(gradients, "ctx")
    squares = lax.psum(jnp.sum(summed * summed), "head")
    update = summed / jnp.sqrt(squares / entry_count + 1e-06)
    return (student, update)


f32, bf16 = jnp.float32, jnp.bfloat16
NN = (((1,), (0,)), ((), ()))
NT = (((1,), (1,)), ((), ()))
TN = (((0,), (0,)), ((), ()))


def mxu(a, b, dims):
    return lax.dot_general(a, b, dims, preferred_element_type=f32)


def split(x, pieces):
    out = []
    for _ in range(pieces):
        piece = x.astype(bf16)
        out.append(piece)
        x = x - piece.astype(f32)
    return out


def cat(parts, axis):
    return jnp.concatenate(parts, axis=axis)


def exact_by_wide(a, b, dims):
    return mxu(cat([a, a], dims[0][0][0]), cat(split(b, 2), dims[0][1][0]), dims)


def wide_by_exact(a, b, dims):
    return mxu(cat(split(a, 2), dims[0][0][0]), cat([b, b], dims[0][1][0]), dims)


def wide_by_wide(a, b, dims):
    a_hi, a_lo = split(a, 2)
    b_hi, b_lo = split(b, 2)
    return mxu(
        cat([a_hi, a_hi, a_lo], dims[0][0][0]), cat([b_hi, b_lo, b_hi], dims[0][1][0]), dims
    )


def half_sum(x, halves):
    return wide_by_exact(x, halves, NN)


def half_softmax(u, is_upper, halves):
    top = jnp.max(jnp.where(is_upper, u, big_negative), axis=-1, keepdims=True)
    low = jnp.max(jnp.where(is_upper, big_negative, u), axis=-1, keepdims=True)
    e = jnp.exp(u - jnp.where(is_upper, top, low))
    return e / half_sum(e, halves)


def remote(src, dst, send_sem, recv_sem, **where):
    return pltpu.make_async_remote_copy(
        src_ref=src,
        dst_ref=dst,
        send_sem=send_sem,
        recv_sem=recv_sem,
        device_id=where,
        device_id_type=pl.DeviceIdType.MESH,
    )


def each(count, body):
    def step(index, carry):
        body(index)
        return carry

    lax.fori_loop(0, count, step, 0)


def head_kernel(
    qt_ref, kvt_ref, w_ref, student_ref, update_ref,
    q_all, kv_all, mix_ref, gat_ref, gat_key_ref, sq_ref, own_ref, sum_ref, pre_ref, pre_norm_ref,
    score_ref, kfeat_ref, gstate_ref, gnorm_ref, state_ref, norm_ref,
    wq_ref, wk_ref, acc_ref, peak_ref, total_ref, gq_ref, gk_ref,
    q_send, q_recv, kv_send, kv_recv, kv_relay, local_sem, st_send, st_recv,
    g_send, g_relay, g_recv, sq_send, sq_recv,
):
    blocks, length, width = qt_ref.shape
    planes = kvt_ref.shape[0]
    group = blocks // planes
    me, side = lax.axis_index("ctx"), lax.axis_index("head")
    plane, spot = me // group, me % group
    features = w_ref.shape[1] // 2
    rows = 2 * length
    steps = blocks // 2

    gats = (gat_ref, gat_key_ref)
    barrier = pltpu.get_barrier_semaphore()

    def greet(t):
        @pl.when(t != me)
        def _():
            pl.semaphore_signal(
                barrier, inc=1, device_id={"ctx": t}, device_id_type=pl.DeviceIdType.MESH
            )

    each(blocks, greet)
    pl.semaphore_signal(
        barrier, inc=1, device_id={"head": 1 - side}, device_id_type=pl.DeviceIdType.MESH
    )
    pl.semaphore_wait(barrier, blocks)

    def kv_column(g):
        return remote(
            kvt_ref.at[g], kv_all.at[me], kv_send.at[g], kv_recv.at[me], ctx=g * group + spot
        )

    def kv_own(r):
        return remote(
            kvt_ref.at[plane], kv_all.at[me], kv_relay.at[plane, r], kv_recv.at[me],
            ctx=plane * group + r,
        )

    def kv_pass(z, r):
        block = z * group + spot
        return remote(
            kv_all.at[block], kv_all.at[block], kv_relay.at[z, r], kv_recv.at[block],
            ctx=plane * group + r,
        )

    def q_copy(t):
        return remote(qt_ref.at[t], q_all.at[me], q_send.at[t], q_recv.at[me], ctx=t)

    def q_arrival(b):
        return remote(qt_ref.at[b], q_all.at[b], q_send.at[b], q_recv.at[b], ctx=b)

    def kv_arrival(b):
        return remote(
            kv_all.at[b], kv_all.at[b], kv_send.at[0], kv_recv.at[b], ctx=b
        )

    def st_copy(b):
        return remote(mix_ref.at[b], student_ref.at[me], st_send.at[b], st_recv.at[me], ctx=b)

    def st_arrival(b):
        return remote(mix_ref.at[b], student_ref.at[b], st_send.at[b], st_recv.at[b], ctx=b)

    def g_column(part, z):
        piece = gats[part].at[me]
        return remote(
            piece, piece, g_send.at[part, z], g_recv.at[me, part], ctx=z * group + spot
        )

    def g_pass(part, z, r):
        block = z * group + spot
        piece = gats[part].at[block]
        return remote(
            piece, piece, g_relay.at[part, z, r], g_recv.at[block, part], ctx=plane * group + r
        )

    def g_arrival(part, b):
        piece = gats[part].at[b]
        return remote(piece, piece, g_send.at[part, 0], g_recv.at[b, part], ctx=b)

    def planes_but_mine(body):
        def one(z):
            @pl.when(z != plane)
            def _():
                body(z)

        each(planes, one)

    def spots_but_mine(body):
        def one(r):
            @pl.when(r != spot)
            def _():
                body(r)

        each(group, one)

    planes_but_mine(lambda g: kv_column(g).start())
    spots_but_mine(lambda r: kv_own(r).start())
    own_kv = pltpu.make_async_copy(kvt_ref.at[plane], kv_all.at[me], local_sem.at[0])
    own_q = pltpu.make_async_copy(qt_ref.at[me], q_all.at[me], local_sem.at[1])
    own_kv.start()
    own_q.start()
    scale = 1.0 / math.sqrt(width)
    lane = lax.broadcasted_iota(jnp.int32, (rows, 2 * features), 1)
    is_upper = lane < features
    row_half = lax.broadcasted_iota(jnp.int32, (2 * features, 2 * features), 0) < features
    col_half = lax.broadcasted_iota(jnp.int32, (2 * features, 2 * features), 1) < features
    halves = jnp.where(row_half == col_half, 1.0, 0.0).astype(bf16)
    w = w_ref[...]
    wq, wk = w[:, :features], w[:, features:]
    wq_ref[...] = cat(split(cat([wq, -wq], 1), 3), 0)
    wk_ref[...] = cat(split(cat([wk, -wk], 1), 3), 0)
    for ref in (state_ref, norm_ref, gq_ref, gk_ref):
        ref[...] = jnp.zeros_like(ref)
    own_kv.wait()
    own_q.wait()

    def pass_on(z):
        kv_arrival(z * group + spot).wait_recv()
        spots_but_mine(lambda r: kv_pass(z, r).start())


    def load(part, i):
        if part == 0:
            return q_all[pl.ds(2 * i, 2)].reshape(rows, width)
        return kv_all[pl.ds(2 * i, 2), part - 1].reshape(rows, width)

    def q_arrived(b):
        @pl.when(b != me)
        def _():
            q_arrival(b).wait_recv()

    def kv_arrived(b):
        @pl.when(b % group != spot)
        def _():
            kv_arrival(b).wait_recv()

    def send_student(b):
        @pl.when(b != me)
        def _():
            st_copy(b).start()

        @pl.when(b == me)
        def _():
            student_ref[me] = mix_ref[me]

    def send_grad(part):
        planes_but_mine(lambda z: g_column(part, z).start())
        spots_but_mine(lambda r: g_pass(part, plane, r).start())

    def relay_grad(part):
        def one(z):
            g_arrival(part, z * group + spot).wait_recv()
            spots_but_mine(lambda r: g_pass(part, z, r).start())

        planes_but_mine(one)

    def key_side(i):
        kv_arrived(2 * i)
        kv_arrived(2 * i + 1)
        k, v = load(1, i), load(2, i)
        kf = half_softmax(mxu(cat([k, k, k], 1), wk_ref[...], NN), is_upper, halves)
        kfeat_ref[i] = kf
        own_ref[2 * i] = wide_by_exact(kf[:length], v[:length], TN)
        own_ref[2 * i + 1] = wide_by_exact(kf[length:], v[length:], TN)
        sum_ref[2 * i] = jnp.sum(kf[:length], axis=0, keepdims=True)
        sum_ref[2 * i + 1] = jnp.sum(kf[length:], axis=0, keepdims=True)

    def push(d):
        q_copy((me + 2 * blocks - 1 - d) % blocks).start()

    each(blocks - 1, push)

    def relay_first(dz):
        pass_on((plane + dz + 1) % planes)

    each(planes - 1, relay_first)

    def stage(dz):
        half = group // 2
        each(half, lambda u: key_side((plane + dz) % planes * half + u))

    each(planes, stage)
    for b in range(2):
        pre_ref[b] = jnp.zeros_like(pre_ref[b])
        pre_norm_ref[b] = jnp.zeros_like(pre_norm_ref[b])

    def prefix(b):
        pre_ref[b + 2] = pre_ref[b + 1] + own_ref[b]
        pre_norm_ref[b + 2] = pre_norm_ref[b + 1] + sum_ref[b]

    each(blocks - 2, prefix)

    def forward(turn, carry):
        i = (me // 2 + turn) % steps
        q_arrived(2 * i)
        q_arrived(2 * i + 1)
        q, v = load(0, i), load(2, i)
        acc_ref[...] = jnp.zeros_like(acc_ref)
        total_ref[...] = jnp.zeros_like(total_ref)
        peak_ref[...] = jnp.full(peak_ref.shape, big_negative, f32)

        def pair_of(part, j):
            return cat([load(part, 2 * j), load(part, 2 * j + 1)], 0)

        def keep(j, s):
            score_ref[2 * j] = s[:, :rows]
            score_ref[2 * j + 1] = s[:, rows:]
            top = jnp.maximum(s[:, :rows], s[:, rows:])
            peak_ref[...] = jnp.maximum(
                peak_ref[...], jnp.maximum(top[:, :length], top[:, length:])
            )

        last = i // 2
        each(last, lambda j: keep(j, mxu(q, pair_of(1, j), NT) * scale))
        s = mxu(q, pair_of(1, last), NT) * scale
        column = lax.broadcasted_iota(jnp.int32, (rows, 2 * rows), 1)
        row = lax.broadcasted_iota(jnp.int32, (rows, 2 * rows), 0)
        keep(last, jnp.where(column <= row + (i - 2 * last) * rows, s, big_negative))
        row_max = jnp.max(peak_ref[...], axis=-1, keepdims=True)

        def weigh(j):
            p0 = jnp.exp(score_ref[2 * j] - row_max)
            p1 = jnp.exp(score_ref[2 * j + 1] - row_max)
            both = p0 + p1
            total_ref[...] += both[:, :length] + both[:, length:]
            p = cat([p0.astype(bf16), p1.astype(bf16)], 1)
            acc_ref[...] += mxu(p, pair_of(2, j), NN)

        each(last + 1, weigh)
        teacher = acc_ref[...] / jnp.sum(total_ref[...], axis=-1, keepdims=True)

        before = jnp.maximum(i - 1, 0)
        s = score_ref[i]
        prev_top = score_ref[before, :length, length:]
        prev_top = jnp.where(i > 0, prev_top, big_negative)
        prev = cat([prev_top, s[length:, :length]], 0)
        own = cat([s[:length, :length], s[length:, length:]], 0)
        win_max = jnp.max(jnp.maximum(prev, own), axis=-1, keepdims=True)
        p_prev, p_own = jnp.exp(prev - win_max), jnp.exp(own - win_max)
        win_den = jnp.sum(p_prev + p_own, axis=-1, keepdims=True)
        b_prev, b_own = p_prev.astype(bf16), p_own.astype(bf16)
        v_before = kv_all[jnp.maximum(2 * i - 1, 0), 1]
        win_num = cat(
            [
                mxu(cat([b_prev[:length], b_own[:length]], 1), cat([v_before, v[:length]], 0), NN),
                mxu(cat([b_prev[length:], b_own[length:]], 1), v, NN),
            ],
            0,
        )

        qf = half_softmax(mxu(cat([q, q, q], 1), wq_ref[...], NN), is_upper, halves)
        state_0, norm_0 = pre_ref[2 * i], pre_norm_ref[2 * i]
        state_1, norm_1 = pre_ref[2 * i + 1], pre_norm_ref[2 * i + 1]

        norm = cat(
            [
                jnp.broadcast_to(norm_0, (length, 2 * features)),
                jnp.broadcast_to(norm_1, (length, 2 * features)),
            ],
            0,
        )
        decay = jnp.exp(-win_max)
        far = cat(
            [wide_by_wide(qf[:length], state_0, NN), wide_by_wide(qf[length:], state_1, NN)], 0
        )
        den = win_den + decay * jnp.sum(qf * norm, axis=-1, keepdims=True)
        mix = (win_num + decay * far) / den
        mix_ref[pl.ds(2 * i, 2)] = mix.astype(bf16).reshape(2, length, width)
        send_student(2 * i)
        send_student(2 * i + 1)
        mismatch = mix - teacher
        g_num = mismatch / den
        g_den = -jnp.sum(mismatch * mix, axis=-1, keepdims=True) / den
        lifted = decay * qf
        gstate_ref[2 * i] = wide_by_wide(lifted[:length], g_num[:length], TN)
        gstate_ref[2 * i + 1] = wide_by_wide(lifted[length:], g_num[length:], TN)
        pulled_norm = lifted * g_den
        gnorm_ref[2 * i] = jnp.sum(pulled_norm[:length], axis=0, keepdims=True)
        gnorm_ref[2 * i + 1] = jnp.sum(pulled_norm[length:], axis=0, keepdims=True)
        g_qf = decay * (
            cat(
                [
                    wide_by_wide(g_num[:length], state_0, NT),
                    wide_by_wide(g_num[length:], state_1, NT),
                ],
                0,
            )
            + norm * g_den
        )
        d_q = qf * (g_qf - half_sum(qf * g_qf, halves))
        gq_ref[...] += wide_by_exact(d_q, q, TN)
        return carry

    lax.fori_loop(0, steps, forward, 0)
    gat_ref[me] = (gq_ref[:features] - gq_ref[features:]).astype(bf16)
    send_grad(0)

    for ref in (state_ref, norm_ref):
        ref[...] = jnp.zeros_like(ref)

    def backward(step, carry):
        i = steps - 1 - step
        k, v, kf = load(1, i), load(2, i), kfeat_ref[i]
        nxt = jnp.minimum(i + 1, steps - 1)
        live = jnp.where(step > 0, 1.0, 0.0)
        later_1, later_n1 = state_ref[...], norm_ref[...]
        later_0 = later_1 + live * gstate_ref[2 * nxt]
        later_n0 = later_n1 + live * gnorm_ref[2 * nxt]
        g_kf = cat(
            [
                exact_by_wide(v[:length], later_0, NT) + later_n0,
                exact_by_wide(v[length:], later_1, NT) + later_n1,
            ],
            0,
        )
        d_k = kf * (g_kf - half_sum(kf * g_kf, halves))
        gk_ref[...] += wide_by_exact(d_k, k, TN)
        state_ref[...] = later_0 + gstate_ref[2 * i + 1]
        norm_ref[...] = later_n0 + gnorm_ref[2 * i + 1]
        return carry

    lax.fori_loop(0, steps, backward, 0)
    gat_key_ref[me] = (gk_ref[:features] - gk_ref[features:]).astype(bf16)
    send_grad(1)
    relay_grad(0)
    relay_grad(1)

    def gathered(b):
        @pl.when(b % group != spot)
        def _():
            g_arrival(0, b).wait_recv()
            g_arrival(1, b).wait_recv()

    each(blocks, gathered)
    squares = jnp.zeros((8, width), f32)
    for b in range(blocks):
        piece = cat([gat_ref[b], gat_key_ref[b]], 0).astype(f32)
        piece = piece.reshape(2 * features // 8, 8, width)
        squares = squares + jnp.sum(piece * piece, axis=0)
    sq_ref[0] = squares
    swap = remote(sq_ref.at[0], sq_ref.at[1], sq_send.at[0], sq_recv.at[0], head=1 - side)
    swap.start()

    def turned(b):
        update_ref[b] = cat([gat_ref[b], gat_key_ref[b]], 0).astype(f32).T

    each(blocks, turned)

    def settle(t):
        @pl.when(t != me)
        def _():
            q_copy(t).wait_send()
            st_copy(t).wait_send()
            st_arrival(t).wait_recv()

    each(blocks, settle)

    def settle_plane(z):
        @pl.when(z != plane)
        def _():
            kv_column(z).wait_send()
            g_column(0, z).wait_send()
            g_column(1, z).wait_send()

        def one(r):
            kv_pass(z, r).wait_send()
            g_pass(0, z, r).wait_send()
            g_pass(1, z, r).wait_send()

        spots_but_mine(one)

    each(planes, settle_plane)
    swap.wait()
    entries = 2 * blocks * width * 2 * features
    total = jnp.sum(sq_ref[0] + sq_ref[1], keepdims=True)
    inverse = 1.0 / jnp.sqrt(total / entries + 1e-06)

    def scaled(b):
        update_ref[b] = update_ref[b] * inverse

    each(blocks, scaled)


def whole_head(qt, kvt, w):
    blocks, length, width = qt.shape
    planes = kvt.shape[0]
    group = blocks // planes
    double = w.shape[1]
    rows, steps = 2 * length, blocks // 2
    vmem, dma = pltpu.VMEM, pltpu.SemaphoreType.DMA
    return pl.pallas_call(
        head_kernel,
        out_shape=(
            jax.ShapeDtypeStruct((blocks, length, width), bf16),
            jax.ShapeDtypeStruct((blocks, width, double), f32),
        ),
        in_specs=[pl.BlockSpec(memory_space=vmem)] * 3,
        out_specs=(pl.BlockSpec(memory_space=vmem),) * 2,
        scratch_shapes=[
            vmem((blocks, length, width), bf16),
            vmem((blocks, 2, length, width), bf16),
            vmem((blocks, length, width), bf16),
            vmem((blocks, double // 2, width), bf16),
            vmem((blocks, double // 2, width), bf16),
            vmem((2, 8, width), f32),
            vmem((blocks, double, width), f32),
            vmem((blocks, 1, double), f32),
            vmem((blocks, double, width), f32),
            vmem((blocks, 1, double), f32),
            vmem((steps, rows, rows), f32),
            vmem((steps, rows, double), f32),
            vmem((blocks, double, width), f32),
            vmem((blocks, 1, double), f32),
            vmem((double, width), f32),
            vmem((1, double), f32),
            vmem((3 * width, double), bf16),
            vmem((3 * width, double), bf16),
            vmem((rows, width), f32),
            vmem((rows, length), f32),
            vmem((rows, length), f32),
            vmem((double, width), f32),
            vmem((double, width), f32),
            dma((blocks,)),
            dma((blocks,)),
            dma((planes,)),
            dma((blocks,)),
            dma((planes, group)),
            dma((2,)),
            dma((blocks,)),
            dma((blocks,)),
            dma((2, planes)),
            dma((2, planes, group)),
            dma((blocks, 2)),
            dma((1,)),
            dma((1,)),
        ],
        compiler_params=pltpu.CompilerParams(
            vmem_limit_bytes=40 * 2**20, collective_id=0, has_side_effects=True
        ),
    )(qt, kvt, w)


def head_shards(queries, keys, values, feature_weight):
    qt = jnp.transpose(queries, (1, 0, 2))
    kvt = jnp.transpose(jnp.stack([keys, values]), (2, 0, 1, 3))
    w = lax.dynamic_index_in_dim(feature_weight, lax.axis_index("ctx"), 0, False)
    student, update = whole_head(qt, kvt, w)
    return (jnp.transpose(student, (1, 0, 2)), update)


def shards(queries, keys, values, feature_weight):
    count = lax.axis_size("ctx")
    width = queries.shape[2]
    fits = queries.shape[1] == count and lax.axis_size("head") == 2 and count % 4 == 0 and count * queries.shape[0] <= 4096
    fits = fits and queries.shape[1] // keys.shape[1] % 2 == 0 and queries.shape[0] == width and feature_weight.shape[2] == width
    body = head_shards if fits else general_shards
    return body(queries, keys, values, feature_weight)


def solution(mesh):
    return jax.shard_map(
        shards,
        mesh=mesh,
        in_specs=(
            P("ctx", "head", None),
            P("ctx", "head", None),
            P("ctx", "head", None),
            P("head", None, None),
        ),
        out_specs=(P("ctx", "head", None), P("head", None, None)),
        check_vma=False,
    )
```
